32 devices in a mesh: batch: 4 (over x, core), tiles: 8 (over z, y).
Axes of the slice: x: 2, y: 2, z: 4, core: 2. Of those that a mesh axis runs over, the one named last changes fastest.
Arguments:
- hidden: bfloat16 [4, 4096, 3072], P('batch', 'tiles'), may hold values from -6 to 6
- frozen_queries: bfloat16 [4, 4096, 1536], P('batch', 'tiles'), may hold values from -108 to 108
- frozen_keys: bfloat16 [4, 4096, 1536], P('batch', 'tiles'), may hold values from -6.09 to 6.09
- frozen_values: bfloat16 [4, 4096, 1536], P('batch', 'tiles'), may hold values from -6 to 6
- reward_output_gradient: bfloat16 [4, 4096, 1536], P('batch', 'tiles'), may hold values from -6 to 6
- truncation_step: int32 [4], P('batch'), may hold values from 0 to 49
- modulation: float32 [50, 2, 3072], replicated, may hold values from -3 to 3
- adapter_down_weight: bfloat16 [3, 3072, 32], replicated, may hold values from -0.109375 to 0.109375
- adapter_up_weight: bfloat16 [3, 32, 1536], replicated, may hold values from -1 to 1
- window: int32 [32, 27], P('tiles'), may hold values from 0 to 1, as said below
Outputs:
- attended: bfloat16 [4, 4096, 1536], P('batch', 'tiles')
- grad_down: float32 [3, 3072, 32], replicated
- grad_up: float32 [3, 32, 1536], replicated
The draws below stay inside these ranges and needn't reach their ends.
Inputs may be any that keep to these rules, and one draw needn't show every extreme that they name: `window`: entry 13, the tile itself, is 1 for every tile.
All inputs are finite; a program needn't handle non-finite values.
Results may differ from the reference program's by a relative error of at most 0.012.
The reference program's roundings to bfloat16 on the way count: a program that leaves them out, or rounds other values in their place, can miss the bound.
Values may be sent and summed in bfloat16 or wider, within the bound.
A program may use at most 192 MiB of HBM per device.

```python
import math
import jax
import jax.numpy as jnp
from jax import lax

MODEL_WIDTH = 3072
HEADS = 12
HEAD = 128
ADAPTER_RANK = 32
TILE = 128
GF = 2
GR = 2
STEPS = 50
HEAD_FEATURES = 1536
SLAB = 512
TOKENS = 4096
TILES_ALL = 32
BATCH = 4
N_TILES = 8


def base_keys(key):
    return jnp.clip(jax.random.normal(jax.random.fold_in(key, 23), (BATCH, TOKENS, HEAD_FEATURES), jnp.float32), -6.0, 6.0)


def draw_hidden(key, part):
    values = jnp.clip(jax.random.normal(jax.random.fold_in(key, 11), (BATCH, TOKENS, MODEL_WIDTH), jnp.float32), -6.0, 6.0)
    return values.astype(jnp.bfloat16)


def draw_frozen_keys(key, part):
    values = base_keys(key)
    return values.astype(jnp.bfloat16)


def draw_frozen_queries(key, part):
    values = jnp.clip(jax.random.normal(jax.random.fold_in(key, 37), (BATCH, TOKENS, HEAD_FEATURES), jnp.float32), -6.0, 6.0)
    return values.astype(jnp.bfloat16)


def draw_window(key, part):
    slab_total = TILES_ALL // (GF * GR)
    levels = jax.random.randint(jax.random.fold_in(key, 5), (slab_total,), 2, 11)
    tile_level = jnp.repeat(levels, GF * GR)
    picks = jax.random.randint(jax.random.fold_in(key, 6), (TILES_ALL, 27), 0, 10)
    chosen = (picks < tile_level[:, None]).astype(jnp.int32)
    centre = (jnp.arange(27) == 13)[None, :]
    return jnp.where(centre, 1, chosen).astype(jnp.int32)


def with_ends(drawn, rng, least, high):
    longest = drawn.shape.index(max(drawn.shape))
    spots = []
    for shift in (0, 1):
        where = [jax.random.randint(jax.random.fold_in(rng, axis), (), 0, length) for axis, length in enumerate(drawn.shape)]
        where[longest] = (where[longest] + shift) % drawn.shape[longest]
        spots.append(tuple(where))
    return drawn.at[spots[0]].set(least).at[spots[1]].set(high)


def block_levels(stream_key, dims, split, least, top_value):
    loudness, own = 1.0, jax.random.fold_in(stream_key, 6)
    for dim, blocks in split:
        draws = jnp.exp(jax.random.uniform(jax.random.fold_in(own, dim), (blocks,), jnp.float32, least / len(split), top_value / len(split)))
        loudness = loudness * jnp.repeat(draws, dims[dim] // blocks).reshape([-1 if axis == dim else 1 for axis in range(len(dims))])
    return loudness


def scatter_about(rng, extent, width, most, cuts=(), held_as=jnp.bfloat16):
    array = jax.random.normal(rng, extent, jnp.float32) * width
    if len(cuts) > 0:
        array = block_levels(rng, extent, cuts, -0.22, 0.18) * array
    return jnp.clip(array, min=-most, max=most).astype(held_as)


def setup_inputs(seed: int = 0) -> dict:
    key_of = jax.random.split(jax.random.key(seed), 11)
    return {
        "hidden": draw_hidden(jax.random.fold_in(key_of[10], 71), 0),
        "frozen_queries": draw_frozen_queries(jax.random.fold_in(key_of[10], 71), 0),
        "frozen_keys": draw_frozen_keys(jax.random.fold_in(key_of[10], 71), 0),
        "frozen_values": scatter_about(key_of[3], (BATCH, TOKENS, HEAD_FEATURES), 1.0, 6.0, ((0, 4), (1, 8))),
        "reward_output_gradient": scatter_about(key_of[4], (BATCH, TOKENS, HEAD_FEATURES), 1.0, 6.0, ((0, 4), (1, 8))),
        "truncation_step": with_ends(jax.random.randint(key_of[5], (BATCH,), 0, STEPS), jax.random.fold_in(key_of[5], 1), 0, STEPS - 1).astype(jnp.int32),
        "modulation": scatter_about(key_of[6], (STEPS, 2, MODEL_WIDTH), 0.5, 3.0, (), jnp.float32),
        "adapter_down_weight": scatter_about(key_of[7], (3, MODEL_WIDTH, ADAPTER_RANK), MODEL_WIDTH ** -0.5, 0.109375),
        "adapter_up_weight": scatter_about(key_of[8], (3, ADAPTER_RANK, HEAD_FEATURES), ADAPTER_RANK ** -0.5, 1.0),
        "window": draw_window(jax.random.fold_in(key_of[10], 71), 0),
    }


precise_variant = lax.Precision.HIGHEST

def allowed_keys(window_rows, slab_index, slab_count):
    per_slab = GF * GR
    query_tile = jnp.arange(per_slab, dtype=jnp.int32)
    key_tile = jnp.arange(3 * per_slab, dtype=jnp.int32)
    key_side = key_tile // per_slab
    key_local = key_tile % per_slab
    frame_step = key_local[None, :] // GR - query_tile[:, None] // GR
    row_step = key_local[None, :] % GR - query_tile[:, None] % GR
    offset_code = (key_side[None, :] * 3 + frame_step + 1) * 3 + row_step + 1
    nearby = (jnp.abs(frame_step) <= 1) & (jnp.abs(row_step) <= 1)
    neighbour = slab_index + key_side - 1
    inside = (neighbour >= 0) & (neighbour < slab_count)
    offsets = jnp.arange(27, dtype=jnp.int32)
    listed = lax.optimization_barrier(jnp.sum(jnp.where(offset_code[:, :, None] == offsets[None, None, :], window_rows[:, None, :], 0), axis=2))
    tile_mask = nearby & inside[None, :] & (listed > 0)
    return jnp.repeat(jnp.repeat(tile_mask, TILE, axis=0), TILE, axis=1)

def modulate(hidden_rows, shift_scale):
    x_full = hidden_rows.astype(jnp.float32)
    row_mean = lax.optimization_barrier(jnp.mean(x_full, axis=1, keepdims=True))
    centred = x_full - row_mean
    variance = lax.optimization_barrier(jnp.mean(centred * centred, axis=1, keepdims=True))
    normed = centred * lax.rsqrt(variance + 1e-06)
    return normed * (1.0 + shift_scale[1][None, :]) + shift_scale[0][None, :]

def attend(queries, key_rows, value_rows, out_grad, allowed):
    scale_root = 1.0 / math.sqrt(HEAD)
    query_heads = queries.reshape(queries.shape[0], HEADS, HEAD).astype(jnp.float32)
    key_heads = key_rows.reshape(key_rows.shape[0], HEADS, HEAD).astype(jnp.float32)
    value_heads = value_rows.reshape(value_rows.shape[0], HEADS, HEAD).astype(jnp.float32)
    grad_heads = out_grad.reshape(out_grad.shape[0], HEADS, HEAD).astype(jnp.float32)
    scores = jnp.einsum('qhe,khe->hqk', query_heads, key_heads, precision=precise_variant) * scale_root
    scores = jnp.where(allowed[None], scores, -1e+30)
    row_max = lax.optimization_barrier(jnp.max(scores, axis=2, keepdims=True))
    weights = jnp.where(allowed[None], jnp.exp(scores - row_max), 0.0)
    totals = lax.optimization_barrier(jnp.sum(weights, axis=2, keepdims=True))
    probs = weights / totals
    probs_low = probs.astype(jnp.bfloat16).astype(jnp.float32)
    attended = jnp.einsum('hqk,khe->qhe', probs_low, value_heads, precision=precise_variant)
    prob_grad = jnp.einsum('qhe,khe->hqk', grad_heads, value_heads, precision=precise_variant)
    centre = lax.optimization_barrier(jnp.sum(probs * prob_grad, axis=2, keepdims=True))
    score_grad = (probs * (prob_grad - centre) * scale_root).astype(jnp.bfloat16).astype(jnp.float32)
    query_grad = jnp.einsum('hqk,khe->qhe', score_grad, key_heads, precision=precise_variant)
    key_grad = jnp.einsum('hqk,qhe->khe', score_grad, query_heads, precision=precise_variant)
    value_grad = jnp.einsum('hqk,qhe->khe', probs_low, grad_heads, precision=precise_variant)
    slab_rows = queries.shape[0]
    return (attended.reshape(slab_rows, HEAD_FEATURES), query_grad.reshape(slab_rows, HEAD_FEATURES), key_grad.reshape(3 * slab_rows, HEAD_FEATURES), value_grad.reshape(3 * slab_rows, HEAD_FEATURES))

def reference(hidden, frozen_queries, frozen_keys, frozen_values, reward_output_gradient, truncation_step, modulation, adapter_down_weight, adapter_up_weight, window):
    per_slab = GF * GR
    expanded_up_weight = adapter_up_weight.astype(jnp.float32)
    down_total = jnp.zeros((3, MODEL_WIDTH, ADAPTER_RANK), jnp.float32)
    up_total = jnp.zeros((3, ADAPTER_RANK, HEAD_FEATURES), jnp.float32)
    outputs = []
    for sample in range(BATCH):
        input_modulated = modulate(hidden[sample], modulation[truncation_step[sample]])
        input_reduced = lax.optimization_barrier(input_modulated.astype(jnp.bfloat16)).astype(jnp.float32)
        reduced_rank_input = jnp.einsum('mx,pxo->pmo', input_reduced, adapter_down_weight.astype(jnp.float32), precision=precise_variant).astype(jnp.bfloat16)
        projected_output = jnp.einsum('bfe,beg->bfg', reduced_rank_input.astype(jnp.float32), expanded_up_weight, precision=precise_variant)
        queries = (frozen_queries[sample] + projected_output[0]).astype(jnp.bfloat16)
        key_rows = (frozen_keys[sample] + projected_output[1]).astype(jnp.bfloat16)
        value_rows = (frozen_values[sample] + projected_output[2]).astype(jnp.bfloat16)
        zero_rows = jnp.zeros((SLAB, HEAD_FEATURES), jnp.bfloat16)
        key_padded = jnp.concatenate([zero_rows, key_rows, zero_rows], axis=0)
        value_padded = jnp.concatenate([zero_rows, value_rows, zero_rows], axis=0)
        out_grad = reward_output_gradient[sample]

        def visit(carry, slab_index):
            key_acc, value_acc = carry
            start = slab_index * SLAB
            query_slab = lax.dynamic_slice_in_dim(queries, start, SLAB, 0)
            key_slab = lax.dynamic_slice_in_dim(key_padded, start, 3 * SLAB, 0)
            value_slab = lax.dynamic_slice_in_dim(value_padded, start, 3 * SLAB, 0)
            grad_slab = lax.dynamic_slice_in_dim(out_grad, start, SLAB, 0)
            window_rows = lax.dynamic_slice_in_dim(window, slab_index * per_slab, per_slab, 0)
            allowed = allowed_keys(window_rows, slab_index, N_TILES)
            attended, query_grad, key_grad, value_grad = attend(query_slab, key_slab, value_slab, grad_slab, allowed)
            key_acc = lax.dynamic_update_slice_in_dim(key_acc, lax.dynamic_slice_in_dim(key_acc, start, 3 * SLAB, 0) + key_grad, start, 0)
            value_acc = lax.dynamic_update_slice_in_dim(value_acc, lax.dynamic_slice_in_dim(value_acc, start, 3 * SLAB, 0) + value_grad, start, 0)
            return ((key_acc, value_acc), (attended.astype(jnp.bfloat16), query_grad))
        zero_acc = jnp.zeros((TOKENS + 2 * SLAB, HEAD_FEATURES), jnp.float32)
        (key_acc, value_acc), (attended_all, query_all) = lax.scan(visit, (zero_acc, zero_acc), jnp.arange(N_TILES, dtype=jnp.int32))
        outputs.append(attended_all.reshape(TOKENS, HEAD_FEATURES))
        grads = jnp.stack([query_all.reshape(TOKENS, HEAD_FEATURES), key_acc[SLAB:SLAB + TOKENS], value_acc[SLAB:SLAB + TOKENS]])
        rank_grads = jnp.einsum('jth,jrh->jtr', grads, expanded_up_weight, precision=precise_variant)
        down_total = down_total + jnp.einsum('td,jtr->jdr', input_modulated, rank_grads, precision=precise_variant)
        up_total = up_total + jnp.einsum('jtr,jth->jrh', reduced_rank_input.astype(jnp.float32), grads, precision=precise_variant)
    norm_factor = 1.0 / math.sqrt(BATCH * TOKENS)
    return (jnp.stack(outputs), down_total * norm_factor, up_total * norm_factor)
```

```python
import functools
import math

import jax
import jax.numpy as jnp
from jax import lax
from jax.experimental import pallas as pl
from jax.experimental.pallas import tpu as pltpu
from jax.sharding import PartitionSpec as P

HEAD = 128
TILE = 128
GF = 2
GR = 2
LANES = 128
ROWS = 16
PARTS = 4
EARLY = 6
AHEAD = 8
BF16 = jnp.bfloat16
F32 = jnp.float32


def dot_nt(a, b):
    return lax.dot_general(
        a, b, (((1,), (1,)), ((), ())), preferred_element_type=jnp.float32
    )


def dot_tn(a, b):
    return lax.dot_general(
        a, b, (((0,), (0,)), ((), ())), preferred_element_type=jnp.float32
    )


def dot_nn(a, b):
    return jnp.dot(a, b, preferred_element_type=jnp.float32)


def remote(src, dst, send, recv, peer):
    return pltpu.make_async_remote_copy(
        src_ref=src, dst_ref=dst, send_sem=send, recv_sem=recv,
        device_id=peer, device_id_type=pl.DeviceIdType.MESH,
    )


class Place:
    def __init__(self, nb, nt):
        self.nb, self.nt = nb, nt
        self.nx, self.nz = nb // 2, nt // 2
        self.nxy = 2 * self.nx
        b, t = lax.axis_index("batch"), lax.axis_index("tiles")
        self.b, self.t = b, t
        self.core, self.x = lax.rem(b, 2), b // 2
        self.y, self.z = lax.rem(t, 2), t // 2

    def core_peer(self):
        return {"batch": self.b + 1 - 2 * self.core}

    def xy_offset(self, d, sign):
        dx, dy = d // 2, d % 2
        x = lax.rem(self.x + sign * dx + self.nx, self.nx)
        return x, lax.rem(self.y + dy, 2)

    def xy_peer(self, d):
        x, y = self.xy_offset(d, 1)
        return {"batch": x * 2 + self.core, "tiles": self.z * 2 + y}

    def xy_index(self, d, sign):
        x, y = self.xy_offset(d, sign)
        return x * 2 + y

    def z_peer(self, e):
        return {"tiles": lax.rem(self.z + e, self.nz) * 2 + self.y}


def share_of(tiles, nb, nt):
    return -(-tiles // (nb * nt))


def sum_shapes(tiles, nb, nt):
    share = share_of(tiles, nb, nt)
    nxy, nz = nb, nt // 2
    quarter = nz * share
    total = nb * nt * share
    dma = pltpu.SemaphoreType.DMA
    return [
        pltpu.VMEM((total, ROWS, LANES), BF16),
        pltpu.VMEM((total // 2, ROWS, LANES), BF16),
        pltpu.VMEM((nxy - 1, quarter, ROWS, LANES), BF16),
        pltpu.VMEM((nxy - 1, quarter, ROWS, LANES), BF16),
        pltpu.VMEM((quarter, ROWS, LANES), F32),
        pltpu.VMEM((nz - 1, share, ROWS, LANES), BF16),
        pltpu.VMEM((nz - 1, share, ROWS, LANES), BF16),
        pltpu.VMEM((total, ROWS, LANES), BF16),
        dma((nxy,)), dma((nxy,)), dma((nxy - 1,)), dma((nxy - 1,)),
        dma((nz - 1,)), dma((nz - 1,)), dma((nz - 1,)), dma((nz - 1,)),
        dma((nxy - 1, nz)), dma((nxy - 1, nz)), dma((nxy, nz)), dma((nxy, nz)),
    ]


class Sum:
    def __init__(self, place, tiles, refs):
        self.place, self.tiles = place, tiles
        (self.terms, self.pair, self.part1, self.got1, self.acc, self.part2, self.got2,
         self.out, self.s0, self.r0, self.s1, self.r1, self.s2, self.r2, self.s3, self.r3,
         self.s4, self.r4, self.s5, self.r5) = refs
        self.share = share_of(tiles, place.nb, place.nt)
        self.quarter = place.nz * self.share
        self.half = place.nxy * self.quarter
        self.mine = place.core * self.half
        self.order = list(range(place.nxy - 1, -1, -1))
        self.sent = []

    def clear(self):
        pad = self.terms.shape[0] - self.tiles
        if pad:
            self.terms[self.tiles:] = jnp.zeros((pad, ROWS, LANES), BF16)

    def go(self, *args):
        copy = remote(*args)
        copy.start()
        self.sent.append(copy)
        return copy

    def pair_start(self):
        p = self.place
        other = (1 - p.core) * self.half
        self.c0 = {}
        for d in self.order:
            q = p.xy_index(d, 1) * self.quarter
            self.c0[d] = self.go(self.terms.at[pl.ds(other + q, self.quarter)],
                                 self.pair.at[pl.ds(q, self.quarter)],
                                 self.s0.at[d], self.r0.at[d], p.core_peer())

    def xy_start(self):
        p = self.place
        self.c1 = {}
        for d in self.order:
            q = p.xy_index(d, 1) * self.quarter
            self.c0[d].wait_recv()
            total = (self.terms[pl.ds(self.mine + q, self.quarter)].astype(F32)
                     + self.pair[pl.ds(q, self.quarter)].astype(F32))
            if d == 0:
                self.acc[...] = total
            else:
                self.part1[d - 1] = total.astype(BF16)
                self.c1[d] = self.go(self.part1.at[d - 1], self.got1.at[d - 1],
                                     self.s1.at[d - 1], self.r1.at[d - 1], p.xy_peer(d))

    def z_start(self):
        p = self.place
        for d in self.order:
            if d:
                self.c1[d].wait_recv()
        total = self.acc[...]
        for d in range(1, p.nxy):
            total = total + self.got1[d - 1].astype(F32)
        self.acc[...] = total
        self.c2 = []
        for e in range(1, p.nz):
            spot = lax.rem(p.z + e, p.nz) * self.share
            self.part2[e - 1] = self.acc[pl.ds(spot, self.share)].astype(BF16)
            self.c2.append(self.go(self.part2.at[e - 1], self.got2.at[e - 1],
                                   self.s2.at[e - 1], self.r2.at[e - 1], p.z_peer(e)))

    def spot(self, d, e):
        p = self.place
        plane = lax.rem(p.z - e + p.nz, p.nz) * self.share
        return self.out.at[pl.ds(self.mine + p.xy_index(d, -1) * self.quarter + plane, self.share)]

    def z_back(self):
        p = self.place
        total = self.acc[pl.ds(p.z * self.share, self.share)]
        for e in range(1, p.nz):
            self.c2[e - 1].wait_recv()
            total = total + self.got2[e - 1].astype(F32)
        mine = self.spot(0, 0)
        mine[...] = total.astype(BF16)
        self.c3 = [self.go(mine, mine, self.s3.at[e - 1], self.r3.at[e - 1], p.z_peer(e))
                   for e in range(1, p.nz)]

    def xy_back(self):
        p = self.place
        self.c4, self.c5 = {}, []
        for e in range(p.nz):
            if e:
                self.c3[e - 1].wait_recv()
            piece = self.spot(0, e)
            for d in self.order:
                if d:
                    self.c4[d, e] = self.go(piece, piece, self.s4.at[d - 1, e],
                                            self.r4.at[d - 1, e], p.xy_peer(d))
            self.c5.append(self.go(piece, piece, self.s5.at[0, e], self.r5.at[0, e],
                                   p.core_peer()))

    def pair_back(self):
        p = self.place
        for e in range(p.nz):
            for d in range(1, p.nxy):
                self.c4[d, e].wait_recv()
                piece = self.spot(d, e)
                self.c5.append(self.go(piece, piece, self.s5.at[d, e], self.r5.at[d, e],
                                       p.core_peer()))

    def finish(self):
        for copy in self.c5:
            copy.wait_recv()

    def drain(self):
        for copy in self.sent:
            copy.wait_send()


def fused_kernel(nb, nt, rank, norm_factor, step_ref, window_ref, hidden_hbm, mod_hbm, down_hbm, up_hbm,
                 fq_hbm, fk_hbm, fv_hbm, g_hbm,
                 att_hbm, gd_ref, gu_ref,
                 x_ref, mod_all, mod_ref, down_ref, up_ref, ups, fq_ref, fk_ref, fv_ref, g_ref,
                 swap_ref, relay_ref, low_ref, low_swap, low_relay, bias_ref, q_ref, kl, vl,
                 probs_s, grad_s, rkv, rq_ref, r_out, r_in, att_ref,
                 load, att_sem, swap_send, swap_recv, relay_send, relay_recv,
                 low_send, low_recv, r_send, r_recv, *sums):
    place = Place(nb, nt)
    t_index, odd = place.t, place.y
    rows, across = fq_ref.shape[1:]
    heads = across // HEAD
    width = x_ref.shape[1]
    half = rows // 2
    chunks = PARTS * heads
    per = len(sums) // 2
    first = Sum(place, (rank // ROWS) * (width // LANES) + (3 * rank // ROWS) * heads, sums[:per])
    later = Sum(place, (2 * rank // ROWS) * (width // LANES), sums[per:])

    partner = {"tiles": t_index + 1 - 2 * odd}
    target = {"tiles": lax.rem(t_index + 2 - 4 * odd + nt, nt)}
    other = {"tiles": lax.rem(t_index - 1 + 2 * odd + nt, nt)}
    even = odd == 0
    relay_in = jnp.where(even, t_index >= 2, t_index < nt - 2)
    relay_out = jnp.where(even, t_index < nt - 2, t_index >= 2)

    blocks = 2 * (rows // TILE)
    block = rows // blocks
    hidden_loads = [
        pltpu.make_async_copy(hidden_hbm.at[0, pl.ds(i * block, block)],
                              x_ref.at[pl.ds(i * block, block)], load.at[i])
        for i in range(blocks)
    ]
    others = [
        pltpu.make_async_copy(src, dst, load.at[blocks + i])
        for i, (src, dst) in enumerate((
            (mod_hbm, mod_all), (down_hbm, down_ref.at[pl.ds(0, 3 * rank)]), (up_hbm, up_ref),
            (fq_hbm, fq_ref), (fk_hbm, fk_ref), (fv_hbm, fv_ref), (g_hbm, g_ref)))
    ]

    barrier = pltpu.get_barrier_semaphore()
    greet = [place.core_peer(), other]
    greet += [place.xy_peer(d) for d in range(1, place.nxy)]
    greet += [place.z_peer(e) for e in range(1, place.nz)]
    for peer in greet:
        pl.semaphore_signal(barrier, inc=1, device_id=peer, device_id_type=pl.DeviceIdType.MESH)
    hidden_loads[0].start()
    for copy in others[:3]:
        copy.start()
    for copy in hidden_loads[1:]:
        copy.start()
    for copy in others[3:]:
        copy.start()

    scale_root = 1.0 / math.sqrt(HEAD)
    scale_two = scale_root * math.log2(math.e)
    per_slab = GF * GR
    sides = (jnp.int32(9), 18 * (1 - odd), 18 * odd)
    for s, side in enumerate(sides):
        for t in range(per_slab):
            for u in range(per_slab):
                code = side + 3 * (u // GR - t // GR + 1) + u % GR - t % GR + 1
                value = jnp.where(window_ref[t, code] > 0, 0.0, -1e30).astype(F32)
                if s == 2:
                    value = jnp.where(relay_in, value, -1e30)
                spot = (s * per_slab + u) * TILE
                bias_ref[t:t + 1, spot:spot + TILE] = jnp.full((1, TILE), value, F32)

    pl.semaphore_wait(barrier, len(greet))

    def swap(h, part):
        src = (fk_hbm, fv_hbm)[part // 2]
        start = (part % 2) * half
        lanes = pl.ds(pl.multiple_of(h * HEAD, HEAD), HEAD)
        c = h * PARTS + part
        return remote(src.at[0, pl.ds(start, half), lanes],
                      swap_ref.at[h, part // 2, pl.ds(start, half)],
                      swap_send.at[c], swap_recv.at[c], partner)

    def chunk(ref, c):
        return ref.at[c // PARTS, lax.rem(c, PARTS) // 2, pl.ds(lax.rem(c, 2) * half, half)]

    def relay(c):
        return remote(chunk(swap_ref, c), chunk(relay_ref, c), relay_send.at[c], relay_recv.at[c],
                      target)

    def pump(c):
        remote(chunk(swap_ref, c), chunk(swap_ref, c), swap_send.at[c], swap_recv.at[c],
               partner).wait_recv()

        @pl.when(relay_out)
        def _():
            relay(c).start()

    for c in range(EARLY):
        swap(c // PARTS, c % PARTS).start()

    @pl.when(jnp.logical_not(relay_in))
    def _():
        low_relay[...] = jnp.zeros_like(low_relay)

        def clear(h, carry):
            relay_ref[h] = jnp.zeros(relay_ref.shape[1:], BF16)
            return carry

        lax.fori_loop(0, heads, clear, 0)
        r_in[1] = jnp.zeros(r_in.shape[1:], BF16)

    first.clear()
    later.clear()
    rq_ref[...] = jnp.zeros_like(rq_ref)
    rkv[...] = jnp.zeros_like(rkv)
    ups[...] = jnp.zeros_like(ups)
    down_ref[3 * rank:] = jnp.zeros((LANES - 3 * rank, width), BF16)

    for copy in others[:3]:
        copy.wait()
    mod_ref[...] = mod_all[step_ref[0]]

    def build(h, carry):
        lanes = pl.ds(pl.multiple_of(h * HEAD, HEAD), HEAD)
        for j in range(3):
            ups[h, j * rank:(j + 1) * rank, j * HEAD:(j + 1) * HEAD] = (
                up_ref[j * rank:(j + 1) * rank, lanes])
        return carry

    lax.fori_loop(0, heads, build, 0)

    def modulate(i, carry):
        span = pl.ds(pl.multiple_of(i * block, block), block)
        pltpu.make_async_copy(hidden_hbm.at[0, span], x_ref.at[span], load.at[i]).wait()
        x = x_ref[span, :].astype(F32)
        mean = jnp.sum(x, axis=1, keepdims=True) * (1.0 / width)
        centred = x - mean
        variance = jnp.sum(centred * centred, axis=1, keepdims=True) * (1.0 / width)
        normed = centred * lax.rsqrt(variance + 1e-06)
        x_low = (normed * (1.0 + mod_ref[1:2, :]) + mod_ref[0:1, :]).astype(BF16)
        x_ref[span, :] = x_low
        low_ref[span, :] = dot_nt(x_low, down_ref[...]).astype(BF16)

        @pl.when(jnp.logical_and(lax.rem(i, 2) == 1, i >= 3))
        def _():
            pump((i - 3) // 2)

        return carry

    lax.fori_loop(0, blocks, modulate, 0)
    pumped = (blocks - 1 - 3) // 2 + 1
    low_first = remote(low_ref, low_swap, low_send.at[0], low_recv.at[0], partner)
    low_next = remote(low_swap, low_relay, low_send.at[1], low_recv.at[1], target)
    low_first.start()
    for c in range(EARLY, 2 * PARTS):
        swap(c // PARTS, c % PARTS).start()

    def send_rest(h, carry):
        for part in range(PARTS):
            swap(h, part).start()
        return carry

    lax.fori_loop(2, heads, send_rest, 0)
    for copy in others[3:]:
        copy.wait()
    for c in range(pumped, EARLY):
        pump(c)
    low_first.wait_recv()

    @pl.when(relay_out)
    def _():
        low_next.start()

    for c in range(EARLY, AHEAD):
        pump(c)

    @pl.when(relay_in)
    def _():
        low_next.wait_recv()

    for s, low in enumerate((low_ref, low_swap, low_relay)):
        kl[s * rows:(s + 1) * rows, HEAD:] = low[...]
        vl[s * rows:(s + 1) * rows, HEAD:] = low[...]

    def reach(h):
        return AHEAD + ((chunks - AHEAD) * h) // (heads - 1)

    up_base = (rank // ROWS) * (width // LANES)

    def att_copy(h):
        lanes = pl.ds(pl.multiple_of(h * HEAD, HEAD), HEAD)
        return pltpu.make_async_copy(att_ref.at[h], att_hbm.at[0, :, lanes], att_sem.at[h])

    def one_head(h, carry):
        @pl.when(relay_in)
        def _():
            for part in range(PARTS):
                relay(h * PARTS + part).wait_recv()

        lanes = pl.ds(pl.multiple_of(h * HEAD, HEAD), HEAD)
        own = dot_nn(low_ref[...], ups[h])
        q_ref[...] = (fq_ref[0, :, lanes].astype(F32) + own[:, 0:HEAD]).astype(BF16)
        kl[0:rows, 0:HEAD] = (fk_ref[0, :, lanes].astype(F32) + own[:, HEAD:2 * HEAD]).astype(BF16)
        vl[0:rows, 0:HEAD] = (fv_ref[0, :, lanes].astype(F32) + own[:, 2 * HEAD:]).astype(BF16)
        for s, (low, part) in enumerate(((low_swap, swap_ref), (low_relay, relay_ref))):
            add = dot_nn(low[...], ups[h, :, HEAD:])
            span = slice((s + 1) * rows, (s + 2) * rows)
            kl[span, 0:HEAD] = (part[h, 0].astype(F32) + add[:, 0:HEAD]).astype(BF16)
            vl[span, 0:HEAD] = (part[h, 1].astype(F32) + add[:, HEAD:]).astype(BF16)
        for t in range(rows // TILE):
            span = slice(t * TILE, (t + 1) * TILE)
            scores = dot_nt(q_ref[span, :], kl[:, 0:HEAD]) * scale_two + bias_ref[t:t + 1, :]
            top = jnp.max(scores, axis=1, keepdims=True)
            weights = jnp.exp2(scores - top)
            inverse = 1.0 / jnp.sum(weights, axis=1, keepdims=True)
            probs = weights * inverse
            prob_grad = dot_nt(g_ref[0, span, lanes], vl[:, 0:HEAD])
            centre = jnp.sum(probs * prob_grad, axis=1, keepdims=True)
            probs_s[span, :] = probs.astype(BF16)
            grad_s[span, :] = (probs * (prob_grad - centre) * scale_root).astype(BF16)
            c = reach(h) + t

            @pl.when(jnp.logical_and(c < reach(h + 1), c < chunks))
            def _():
                pump(c)

        q_all = q_ref[...]
        g_all = g_ref[0, :, lanes]
        q_up = dot_nt(up_ref[rank:2 * rank, lanes], q_all).astype(BF16)
        g_up = dot_nt(up_ref[2 * rank:3 * rank, lanes], g_all).astype(BF16)
        rkv[0:rank, :] += dot_nn(q_up, grad_s[...])
        rkv[rank:2 * rank, :] += dot_nn(g_up, probs_s[...])
        att = dot_nn(probs_s[...], vl[...])
        att_ref[h] = att[:, 0:HEAD].astype(BF16)
        att_copy(h).start()
        low_v = att[:, HEAD:].astype(BF16)
        dq = dot_nn(grad_s[...], kl[...])
        dq_low = dq[:, 0:HEAD].astype(BF16)
        low_k = dq[:, HEAD:].astype(BF16)
        rq_ref[...] += dot_nt(up_ref[0:rank, lanes], dq_low)
        ups_terms = (dot_tn(low_ref[...], dq_low), dot_tn(low_k, q_all), dot_tn(low_v, g_all))
        for j, term in enumerate(ups_terms):
            for r in range(rank // ROWS):
                start = j * rank + r * ROWS
                spot = up_base + h * (3 * rank // ROWS) + start // ROWS
                first.terms[spot] = (term[start:start + ROWS] * norm_factor).astype(BF16)
        return carry

    lax.fori_loop(0, heads, one_head, 0)

    returns = []
    for s, peer in enumerate((partner, other)):
        r_out[s] = rkv[:, (s + 1) * rows:(s + 2) * rows].astype(BF16)
        returns.append(remote(r_out.at[s], r_in.at[s], r_send.at[s], r_recv.at[s], peer))
    returns[0].start()

    @pl.when(relay_in)
    def _():
        returns[1].start()

    def down_dot(total, grads, count):
        def columns(i, carry):
            lanes = pl.ds(pl.multiple_of(i * 2 * LANES, 2 * LANES), 2 * LANES)
            term = dot_nn(grads, x_ref[:, lanes]) * norm_factor
            for l in range(2):
                for r in range(count):
                    total.terms[(i * 2 + l) * count + r] = (
                        term[r * ROWS:(r + 1) * ROWS, l * LANES:(l + 1) * LANES].astype(BF16))
            return carry

        lax.fori_loop(0, width // (2 * LANES), columns, 0)

    down_dot(first, rq_ref[...].astype(BF16), rank // ROWS)
    first.pair_start()
    returns[0].wait_recv()

    @pl.when(relay_in)
    def _():
        returns[1].wait_recv()

    owned = rkv[:, 0:rows] + r_in[0].astype(F32) + r_in[1].astype(F32)
    down_dot(later, owned.astype(BF16), 2 * rank // ROWS)
    later.pair_start()
    first.xy_start()
    later.xy_start()
    first.z_start()
    later.z_start()
    first.z_back()
    later.z_back()
    first.xy_back()
    later.xy_back()
    first.pair_back()
    later.pair_back()
    first.finish()

    def unpack_first(i, carry):
        lanes = pl.ds(pl.multiple_of(i * LANES, LANES), LANES)
        for r in range(rank // ROWS):
            gd_ref[r * ROWS:(r + 1) * ROWS, lanes] = first.out[i * (rank // ROWS) + r]
        return carry

    lax.fori_loop(0, width // LANES, unpack_first, 0)

    def unpack_up(h, carry):
        lanes = pl.ds(pl.multiple_of(h * LANES, LANES), LANES)
        for r in range(3 * rank // ROWS):
            gu_ref[r * ROWS:(r + 1) * ROWS, lanes] = first.out[up_base + h * (3 * rank // ROWS) + r]
        return carry

    lax.fori_loop(0, heads, unpack_up, 0)
    later.finish()

    def unpack_later(i, carry):
        lanes = pl.ds(pl.multiple_of(i * LANES, LANES), LANES)
        for r in range(2 * rank // ROWS):
            gd_ref[rank + r * ROWS:rank + (r + 1) * ROWS, lanes] = (
                later.out[i * (2 * rank // ROWS) + r])
        return carry

    lax.fori_loop(0, width // LANES, unpack_later, 0)

    low_first.wait_send()

    @pl.when(relay_out)
    def _():
        low_next.wait_send()

    def swap_sent(h, carry):
        for part in range(PARTS):
            swap(h, part).wait_send()
        return carry

    lax.fori_loop(0, heads, swap_sent, 0)

    @pl.when(relay_out)
    def _():
        lax.fori_loop(0, chunks, lambda c, carry: (relay(c).wait_send(), carry)[1], 0)

    returns[0].wait_send()

    @pl.when(relay_in)
    def _():
        returns[1].wait_send()

    lax.fori_loop(0, heads, lambda h, carry: (att_copy(h).wait(), carry)[1], 0)
    first.drain()
    later.drain()


def fused(nb, nt, norm_factor, step, window, hidden, modulation, down, up, fq, fk, fv, g):
    _, rows, width = hidden.shape
    across = fq.shape[2]
    heads = across // HEAD
    rank = up.shape[0] // 3
    dma = pltpu.SemaphoreType.DMA
    vmem = pltpu.VMEM
    smem = pl.BlockSpec(memory_space=pltpu.SMEM)
    anywhere = pl.BlockSpec(memory_space=pl.ANY)
    whole = pl.BlockSpec(memory_space=pltpu.VMEM)
    chunks = PARTS * heads
    blocks = 2 * (rows // TILE)
    first_tiles = (rank // ROWS) * (width // LANES) + (3 * rank // ROWS) * heads
    later_tiles = (2 * rank // ROWS) * (width // LANES)
    return pl.pallas_call(
        functools.partial(fused_kernel, nb, nt, rank, norm_factor),
        out_shape=[
            jax.ShapeDtypeStruct((1, rows, across), BF16),
            jax.ShapeDtypeStruct((3 * rank, width), BF16),
            jax.ShapeDtypeStruct((3 * rank, across), BF16),
        ],
        in_specs=[smem, smem] + [anywhere] * 8,
        out_specs=[anywhere, whole, whole],
        scratch_shapes=[
            vmem((rows, width), BF16), vmem(modulation.shape, F32), vmem((2, width), F32),
            vmem((LANES, width), BF16), vmem(up.shape, BF16), vmem((heads, LANES, 3 * HEAD), BF16),
            vmem(fq.shape, BF16), vmem(fq.shape, BF16), vmem(fq.shape, BF16), vmem(fq.shape, BF16),
            vmem((heads, 2, rows, HEAD), BF16), vmem((heads, 2, rows, HEAD), BF16),
            vmem((rows, LANES), BF16), vmem((rows, LANES), BF16), vmem((rows, LANES), BF16),
            vmem((8, 3 * rows), F32), vmem((rows, HEAD), BF16),
            vmem((3 * rows, 2 * HEAD), BF16), vmem((3 * rows, 2 * HEAD), BF16),
            vmem((rows, 3 * rows), BF16), vmem((rows, 3 * rows), BF16),
            vmem((2 * rank, 3 * rows), F32), vmem((rank, rows), F32),
            vmem((2, 2 * rank, rows), BF16), vmem((2, 2 * rank, rows), BF16),
            vmem((heads, rows, HEAD), BF16),
            dma((blocks + 7,)), dma((heads,)),
            dma((chunks,)), dma((chunks,)), dma((chunks,)), dma((chunks,)),
            dma((2,)), dma((2,)), dma((2,)), dma((2,)),
        ] + sum_shapes(first_tiles, nb, nt) + sum_shapes(later_tiles, nb, nt),
        compiler_params=pltpu.CompilerParams(
            collective_id=0, has_side_effects=True, vmem_limit_bytes=60 << 20
        ),
        name="fused",
    )(step, window, hidden, modulation, down, up, fq, fk, fv, g)


def per_device(
    hidden,
    frozen_queries,
    frozen_keys,
    frozen_values,
    reward_output_gradient,
    truncation_step,
    modulation,
    adapter_down_weight,
    adapter_up_weight,
    window,
):
    slab_rows, width = hidden.shape[1:]
    across = frozen_queries.shape[2]
    rank = adapter_up_weight.shape[1]
    nb, nt = lax.axis_size("batch"), lax.axis_size("tiles")
    norm_factor = 1.0 / math.sqrt(hidden.shape[0] * nb * slab_rows * nt)
    down = adapter_down_weight.transpose(0, 2, 1).reshape(3 * rank, width)
    up = adapter_up_weight.reshape(3 * rank, across)
    attended, grad_down, grad_up = fused(
        nb, nt, norm_factor, truncation_step, window, hidden, modulation, down, up,
        frozen_queries, frozen_keys, frozen_values, reward_output_gradient,
    )
    grad_down = grad_down.astype(jnp.float32).reshape(3, rank, width).transpose(0, 2, 1)
    grad_up = grad_up.astype(jnp.float32).reshape(3, rank, across)
    return (attended, grad_down, grad_up)


def solution(mesh):
    placed = (
        P("batch", "tiles", None),
        P("batch", "tiles", None),
        P("batch", "tiles", None),
        P("batch", "tiles", None),
        P("batch", "tiles", None),
        P("batch"),
        P(),
        P(),
        P(),
        P("tiles", None),
    )
    return jax.shard_map(
        per_device,
        mesh=mesh,
        in_specs=placed,
        out_specs=(P("batch", "tiles", None), P(), P()),
        check_vma=False,
    )
```

```python
import functools
import math

import jax
import jax.numpy as jnp
from jax import lax
from jax.experimental import pallas as pl
from jax.experimental.pallas import tpu as pltpu
from jax.sharding import PartitionSpec as P

HEAD = 128
TILE = 128
GF = 2
GR = 2
LANES = 128
ROWS = 16
PARTS = 4
EARLY = 4
BF16 = jnp.bfloat16
F32 = jnp.float32


def dot_nt(a, b):
    return lax.dot_general(
        a, b, (((1,), (1,)), ((), ())), preferred_element_type=jnp.float32
    )


def dot_tn(a, b):
    return lax.dot_general(
        a, b, (((0,), (0,)), ((), ())), preferred_element_type=jnp.float32
    )


def dot_nn(a, b):
    return jnp.dot(a, b, preferred_element_type=jnp.float32)


def remote(src, dst, send, recv, peer):
    return pltpu.make_async_remote_copy(
        src_ref=src, dst_ref=dst, send_sem=send, recv_sem=recv,
        device_id=peer, device_id_type=pl.DeviceIdType.MESH,
    )


class Place:
    def __init__(self, nb, nt):
        self.nb, self.nt = nb, nt
        self.nx, self.nz = nb // 2, nt // 2
        self.nxy = 2 * self.nx
        b, t = lax.axis_index("batch"), lax.axis_index("tiles")
        self.b, self.t = b, t
        self.core, self.x = lax.rem(b, 2), b // 2
        self.y, self.z = lax.rem(t, 2), t // 2

    def core_peer(self):
        return {"batch": self.b + 1 - 2 * self.core}

    def xy_offset(self, d, sign):
        dx, dy = d // 2, d % 2
        x = lax.rem(self.x + sign * dx + self.nx, self.nx)
        return x, lax.rem(self.y + dy, 2)

    def xy_peer(self, d):
        x, y = self.xy_offset(d, 1)
        return {"batch": x * 2 + self.core, "tiles": self.z * 2 + y}

    def xy_index(self, d, sign):
        x, y = self.xy_offset(d, sign)
        return x * 2 + y

    def z_peer(self, e):
        return {"tiles": lax.rem(self.z + e, self.nz) * 2 + self.y}


def share_of(tiles, nb, nt):
    return -(-tiles // (nb * nt))


def sum_shapes(tiles, nb, nt):
    share = share_of(tiles, nb, nt)
    nxy, nz = nb, nt // 2
    quarter = nz * share
    total = nb * nt * share
    dma = pltpu.SemaphoreType.DMA
    return [
        pltpu.VMEM((total, ROWS, LANES), BF16),
        pltpu.VMEM((total // 2, ROWS, LANES), BF16),
        pltpu.VMEM((nxy - 1, quarter, ROWS, LANES), BF16),
        pltpu.VMEM((nxy - 1, quarter, ROWS, LANES), BF16),
        pltpu.VMEM((quarter, ROWS, LANES), F32),
        pltpu.VMEM((nz - 1, share, ROWS, LANES), BF16),
        pltpu.VMEM((nz - 1, share, ROWS, LANES), BF16),
        pltpu.VMEM((total, ROWS, LANES), BF16),
        dma((nxy,)), dma((nxy,)), dma((nxy - 1,)), dma((nxy - 1,)),
        dma((nz - 1,)), dma((nz - 1,)), dma((nz - 1,)), dma((nz - 1,)),
        dma((nxy - 1, nz)), dma((nxy - 1, nz)), dma((nxy, nz)), dma((nxy, nz)),
    ]


class Sum:
    def __init__(self, place, tiles, refs):
        self.place, self.tiles = place, tiles
        (self.terms, self.pair, self.part1, self.got1, self.acc, self.part2, self.got2,
         self.out, self.s0, self.r0, self.s1, self.r1, self.s2, self.r2, self.s3, self.r3,
         self.s4, self.r4, self.s5, self.r5) = refs
        self.share = share_of(tiles, place.nb, place.nt)
        self.quarter = place.nz * self.share
        self.half = place.nxy * self.quarter
        self.mine = place.core * self.half
        self.order = list(range(place.nxy - 1, -1, -1))
        self.sent = []

    def clear(self):
        pad = self.terms.shape[0] - self.tiles
        if pad:
            self.terms[self.tiles:] = jnp.zeros((pad, ROWS, LANES), BF16)

    def go(self, *args):
        copy = remote(*args)
        copy.start()
        self.sent.append(copy)
        return copy

    def pair_start(self):
        p = self.place
        other = (1 - p.core) * self.half
        self.c0 = {}
        for d in self.order:
            q = p.xy_index(d, 1) * self.quarter
            self.c0[d] = self.go(self.terms.at[pl.ds(other + q, self.quarter)],
                                 self.pair.at[pl.ds(q, self.quarter)],
                                 self.s0.at[d], self.r0.at[d], p.core_peer())

    def xy_start(self):
        p = self.place
        self.c1 = {}
        for d in self.order:
            q = p.xy_index(d, 1) * self.quarter
            self.c0[d].wait_recv()
            total = (self.terms[pl.ds(self.mine + q, self.quarter)].astype(F32)
                     + self.pair[pl.ds(q, self.quarter)].astype(F32))
            if d == 0:
                self.acc[...] = total
            else:
                self.part1[d - 1] = total.astype(BF16)
                self.c1[d] = self.go(self.part1.at[d - 1], self.got1.at[d - 1],
                                     self.s1.at[d - 1], self.r1.at[d - 1], p.xy_peer(d))

    def z_start(self):
        p = self.place
        for d in self.order:
            if d:
                self.c1[d].wait_recv()
        total = self.acc[...]
        for d in range(1, p.nxy):
            total = total + self.got1[d - 1].astype(F32)
        self.acc[...] = total
        self.c2 = []
        for e in range(1, p.nz):
            spot = lax.rem(p.z + e, p.nz) * self.share
            self.part2[e - 1] = self.acc[pl.ds(spot, self.share)].astype(BF16)
            self.c2.append(self.go(self.part2.at[e - 1], self.got2.at[e - 1],
                                   self.s2.at[e - 1], self.r2.at[e - 1], p.z_peer(e)))

    def spot(self, d, e):
        p = self.place
        plane = lax.rem(p.z - e + p.nz, p.nz) * self.share
        return self.out.at[pl.ds(self.mine + p.xy_index(d, -1) * self.quarter + plane, self.share)]

    def z_back(self):
        p = self.place
        total = self.acc[pl.ds(p.z * self.share, self.share)]
        for e in range(1, p.nz):
            self.c2[e - 1].wait_recv()
            total = total + self.got2[e - 1].astype(F32)
        mine = self.spot(0, 0)
        mine[...] = total.astype(BF16)
        self.c3 = [self.go(mine, mine, self.s3.at[e - 1], self.r3.at[e - 1], p.z_peer(e))
                   for e in range(1, p.nz)]

    def xy_back(self):
        p = self.place
        self.c4, self.c5 = {}, []
        for e in range(p.nz):
            if e:
                self.c3[e - 1].wait_recv()
            piece = self.spot(0, e)
            for d in self.order:
                if d:
                    self.c4[d, e] = self.go(piece, piece, self.s4.at[d - 1, e],
                                            self.r4.at[d - 1, e], p.xy_peer(d))
            self.c5.append(self.go(piece, piece, self.s5.at[0, e], self.r5.at[0, e],
                                   p.core_peer()))

    def pair_back(self):
        p = self.place
        for e in range(p.nz):
            for d in range(1, p.nxy):
                self.c4[d, e].wait_recv()
                piece = self.spot(d, e)
                self.c5.append(self.go(piece, piece, self.s5.at[d, e], self.r5.at[d, e],
                                       p.core_peer()))

    def finish(self):
        for copy in self.c5:
            copy.wait_recv()

    def drain(self):
        for copy in self.sent:
            copy.wait_send()


def fused_kernel(nb, nt, rank, norm_factor, step_ref, window_ref, hidden_hbm, mod_hbm, down_hbm, up_hbm,
                 fq_hbm, fk_hbm, fv_hbm, g_hbm,
                 att_hbm, gd_ref, gu_ref,
                 x_ref, mod_all, mod_ref, down_ref, up_ref, ups, fq_ref, fk_ref, fv_ref, g_ref,
                 swap_ref, relay_ref, low_pack, low_got, low_ref, low_swap, low_relay, bias_ref, q_ref, kl, vl,
                 probs_s, grad_s, rkv, rq_ref, r_out, r_in, att_ref,
                 load, att_sem, swap_send, swap_recv, relay_send, relay_recv,
                 low_send, low_recv, r_send, r_recv, *sums):
    place = Place(nb, nt)
    t_index, odd = place.t, place.y
    rows, across = fq_ref.shape[1:]
    heads = across // HEAD
    width = x_ref.shape[1]
    half = rows // 2
    chunks = PARTS * heads
    per = len(sums) // 2
    first = Sum(place, (rank // ROWS) * (width // LANES) + (3 * rank // ROWS) * heads, sums[:per])
    later = Sum(place, (2 * rank // ROWS) * (width // LANES), sums[per:])

    partner = {"tiles": t_index + 1 - 2 * odd}
    target = {"tiles": lax.rem(t_index + 2 - 4 * odd + nt, nt)}
    other = {"tiles": lax.rem(t_index - 1 + 2 * odd + nt, nt)}
    even = odd == 0
    relay_in = jnp.where(even, t_index >= 2, t_index < nt - 2)
    relay_out = jnp.where(even, t_index < nt - 2, t_index >= 2)

    blocks = 2 * (rows // TILE)
    block = rows // blocks
    hidden_loads = [
        pltpu.make_async_copy(hidden_hbm.at[0, pl.ds(i * block, block)],
                              x_ref.at[pl.ds(i * block, block)], load.at[i])
        for i in range(blocks)
    ]
    others = [
        pltpu.make_async_copy(src, dst, load.at[blocks + i])
        for i, (src, dst) in enumerate((
            (mod_hbm, mod_all), (down_hbm, down_ref.at[pl.ds(0, 3 * rank)]),
            (down_hbm.at[pl.ds(rank, 2 * rank)], down_ref.at[pl.ds(LANES, 2 * rank)]),
            (down_hbm.at[pl.ds(rank, 2 * rank)], down_ref.at[pl.ds(LANES + 2 * rank, 2 * rank)]),
            (up_hbm, up_ref),
            (fq_hbm, fq_ref), (fk_hbm, fk_ref), (fv_hbm, fv_ref), (g_hbm, g_ref)))
    ]

    barrier = pltpu.get_barrier_semaphore()
    greet = [place.core_peer(), other]
    greet += [place.xy_peer(d) for d in range(1, place.nxy)]
    greet += [place.z_peer(e) for e in range(1, place.nz)]
    for peer in greet:
        pl.semaphore_signal(barrier, inc=1, device_id=peer, device_id_type=pl.DeviceIdType.MESH)
    hidden_loads[0].start()
    for copy in others[:4]:
        copy.start()
    for copy in hidden_loads[1:]:
        copy.start()
    for copy in others[4:]:
        copy.start()

    scale_root = 1.0 / math.sqrt(HEAD)
    scale_two = scale_root * math.log2(math.e)
    per_slab = GF * GR
    sides = (jnp.int32(9), 18 * (1 - odd), 18 * odd)
    for s, side in enumerate(sides):
        for t in range(per_slab):
            for u in range(per_slab):
                code = side + 3 * (u // GR - t // GR + 1) + u % GR - t % GR + 1
                value = jnp.where(window_ref[t, code] > 0, 0.0, -1e30).astype(F32)
                if s == 2:
                    value = jnp.where(relay_in, value, -1e30)
                spot = (s * per_slab + u) * TILE
                bias_ref[t:t + 1, spot:spot + TILE] = jnp.full((1, TILE), value, F32)

    pl.semaphore_wait(barrier, len(greet))

    def swap(h, part):
        src = (fk_hbm, fv_hbm)[part // 2]
        start = (part % 2) * half
        lanes = pl.ds(pl.multiple_of(h * HEAD, HEAD), HEAD)
        c = h * PARTS + part
        return remote(src.at[0, pl.ds(start, half), lanes],
                      swap_ref.at[h, part // 2, pl.ds(start, half)],
                      swap_send.at[c], swap_recv.at[c], partner)

    def chunk(ref, c):
        return ref.at[c // PARTS, lax.rem(c, PARTS) // 2, pl.ds(lax.rem(c, 2) * half, half)]

    def relay(c):
        return remote(chunk(swap_ref, c), chunk(relay_ref, c), relay_send.at[c], relay_recv.at[c],
                      target)

    def pump(c):
        remote(chunk(swap_ref, c), chunk(swap_ref, c), swap_send.at[c], swap_recv.at[c],
               partner).wait_recv()

        @pl.when(relay_out)
        def _():
            relay(c).start()

    for c in range(EARLY):
        swap(c // PARTS, c % PARTS).start()

    @pl.when(jnp.logical_not(relay_in))
    def _():
        low_relay[...] = jnp.zeros_like(low_relay)

        def clear(h, carry):
            relay_ref[h] = jnp.zeros(relay_ref.shape[1:], BF16)
            return carry

        lax.fori_loop(0, heads, clear, 0)
        r_in[1] = jnp.zeros(r_in.shape[1:], BF16)

    first.clear()
    later.clear()
    rq_ref[...] = jnp.zeros_like(rq_ref)
    rkv[...] = jnp.zeros_like(rkv)
    ups[...] = jnp.zeros_like(ups)
    down_ref[3 * rank:LANES] = jnp.zeros((LANES - 3 * rank, width), BF16)

    for copy in others[:4]:
        copy.wait()
    mod_ref[...] = mod_all[step_ref[0]]

    def low_copy(g):
        return remote(low_pack.at[g], low_got.at[g], low_send.at[g], low_recv.at[g], partner)

    def low_next(g):
        return remote(low_got.at[g], low_got.at[2 + g], low_send.at[2 + g], low_recv.at[2 + g],
                      target)

    def modulate(i, carry):
        span = pl.ds(pl.multiple_of(i * block, block), block)
        pltpu.make_async_copy(hidden_hbm.at[0, span], x_ref.at[span], load.at[i]).wait()
        x = x_ref[span, :].astype(F32)
        mean = jnp.sum(x, axis=1, keepdims=True) * (1.0 / width)
        centred = x - mean
        variance = jnp.sum(centred * centred, axis=1, keepdims=True) * (1.0 / width)
        normed = centred * lax.rsqrt(variance + 1e-06)
        x_low = (normed * (1.0 + mod_ref[1:2, :]) + mod_ref[0:1, :]).astype(BF16)
        x_ref[span, :] = x_low
        low = dot_nt(x_low, down_ref[...]).astype(BF16)
        low_ref[span, :] = low[:, 0:LANES]
        inner = pl.ds(pl.multiple_of(lax.rem(i, blocks // 4) * block, block), block)
        group = i // (blocks // 2)
        second = lax.rem(i // (blocks // 4), 2) == 1

        @pl.when(jnp.logical_not(second))
        def _():
            low_pack[group, inner, 0:2 * rank] = low[:, LANES:LANES + 2 * rank]

        @pl.when(second)
        def _():
            low_pack[group, inner, 2 * rank:] = low[:, LANES + 2 * rank:]

        @pl.when(lax.rem(i, blocks // 2) == blocks // 2 - 1)
        def _():
            low_copy(group).start()

        return carry

    lax.fori_loop(0, blocks, modulate, 0)
    for c in range(EARLY, 2 * PARTS):
        swap(c // PARTS, c % PARTS).start()

    def send_rest(h, carry):
        for part in range(PARTS):
            swap(h, part).start()
        return carry

    lax.fori_loop(2, heads, send_rest, 0)
    pump(0)
    pump(1)
    for copy in others[4:]:
        copy.wait()

    def build(h, carry):
        lanes = pl.ds(pl.multiple_of(h * HEAD, HEAD), HEAD)
        for j in range(3):
            ups[h, j * rank:(j + 1) * rank, j * HEAD:(j + 1) * HEAD] = (
                up_ref[j * rank:(j + 1) * rank, lanes])
        return carry

    lax.fori_loop(0, heads, build, 0)
    pump(2)
    pump(3)
    for g in range(2):
        low_copy(g).wait_recv()

        @pl.when(relay_out)
        def _(g=g):
            low_next(g).start()

    row = lax.broadcasted_iota(jnp.int32, (LANES, LANES), 0)
    lane = lax.broadcasted_iota(jnp.int32, (LANES, LANES), 1)
    inside = jnp.logical_and(lane >= rank, lane < 3 * rank)

    def unpack_low(s, dst):
        quarter = rows // 4
        for part in range(2):
            pick = jnp.logical_and(inside, row == lane - rank + part * 2 * rank)
            select = jnp.where(pick, 1.0, 0.0).astype(BF16)
            for g in range(2):
                start = (2 * g + part) * quarter
                dst[start:start + quarter, :] = dot_nn(low_got[2 * s + g], select).astype(BF16)

    unpack_low(0, low_swap)

    @pl.when(relay_in)
    def _():
        for g in range(2):
            low_next(g).wait_recv()
        unpack_low(1, low_relay)

    for s, low in enumerate((low_ref, low_swap, low_relay)):
        kl[s * rows:(s + 1) * rows, HEAD:] = low[...]
        vl[s * rows:(s + 1) * rows, HEAD:] = low[...]

    up_base = (rank // ROWS) * (width // LANES)

    def att_copy(h):
        lanes = pl.ds(pl.multiple_of(h * HEAD, HEAD), HEAD)
        return pltpu.make_async_copy(att_ref.at[h], att_hbm.at[0, :, lanes], att_sem.at[h])

    def pump_next(h, part):
        @pl.when(h + 1 < heads)
        def _():
            pump((h + 1) * PARTS + part)

    def one_head(h, carry):
        pump_next(h, 0)
        pump_next(h, 1)

        @pl.when(relay_in)
        def _():
            for part in range(PARTS):
                relay(h * PARTS + part).wait_recv()

        lanes = pl.ds(pl.multiple_of(h * HEAD, HEAD), HEAD)
        own = dot_nn(low_ref[...], ups[h])
        q_ref[...] = (fq_ref[0, :, lanes].astype(F32) + own[:, 0:HEAD]).astype(BF16)
        kl[0:rows, 0:HEAD] = (fk_ref[0, :, lanes].astype(F32) + own[:, HEAD:2 * HEAD]).astype(BF16)
        vl[0:rows, 0:HEAD] = (fv_ref[0, :, lanes].astype(F32) + own[:, 2 * HEAD:]).astype(BF16)
        for s, (low, part) in enumerate(((low_swap, swap_ref), (low_relay, relay_ref))):
            add = dot_nn(low[...], ups[h, :, HEAD:])
            span = slice((s + 1) * rows, (s + 2) * rows)
            kl[span, 0:HEAD] = (part[h, 0].astype(F32) + add[:, 0:HEAD]).astype(BF16)
            vl[span, 0:HEAD] = (part[h, 1].astype(F32) + add[:, HEAD:]).astype(BF16)
        for t in range(rows // TILE):
            span = slice(t * TILE, (t + 1) * TILE)
            scores = dot_nt(q_ref[span, :], kl[:, 0:HEAD]) * scale_two + bias_ref[t:t + 1, :]
            top = jnp.max(scores, axis=1, keepdims=True)
            weights = jnp.exp2(scores - top)
            inverse = 1.0 / jnp.sum(weights, axis=1, keepdims=True)
            probs = weights * inverse
            prob_grad = dot_nt(g_ref[0, span, lanes], vl[:, 0:HEAD])
            centre = jnp.sum(probs * prob_grad, axis=1, keepdims=True)
            probs_s[span, :] = probs.astype(BF16)
            grad_s[span, :] = (probs * (prob_grad - centre) * scale_root).astype(BF16)
            if t % 2 == 0:
                pump_next(h, 2 + t // 2)

        q_all = q_ref[...]
        g_all = g_ref[0, :, lanes]
        q_up = dot_nt(up_ref[rank:2 * rank, lanes], q_all).astype(BF16)
        g_up = dot_nt(up_ref[2 * rank:3 * rank, lanes], g_all).astype(BF16)
        rkv[0:rank, :] += dot_nn(q_up, grad_s[...])
        rkv[rank:2 * rank, :] += dot_nn(g_up, probs_s[...])
        att = dot_nn(probs_s[...], vl[...])
        att_ref[h] = att[:, 0:HEAD].astype(BF16)
        att_copy(h).start()
        low_v = att[:, HEAD:].astype(BF16)
        dq = dot_nn(grad_s[...], kl[...])
        dq_low = dq[:, 0:HEAD].astype(BF16)
        low_k = dq[:, HEAD:].astype(BF16)
        rq_ref[...] += dot_nt(up_ref[0:rank, lanes], dq_low)
        ups_terms = (dot_tn(low_ref[...], dq_low), dot_tn(low_k, q_all), dot_tn(low_v, g_all))
        for j, term in enumerate(ups_terms):
            for r in range(rank // ROWS):
                start = j * rank + r * ROWS
                spot = up_base + h * (3 * rank // ROWS) + start // ROWS
                first.terms[spot] = (term[start:start + ROWS] * norm_factor).astype(BF16)
        return carry

    lax.fori_loop(0, heads, one_head, 0)

    returns = []
    for s, peer in enumerate((partner, other)):
        r_out[s] = rkv[:, (s + 1) * rows:(s + 2) * rows].astype(BF16)
        returns.append(remote(r_out.at[s], r_in.at[s], r_send.at[s], r_recv.at[s], peer))
    returns[0].start()

    @pl.when(relay_in)
    def _():
        returns[1].start()

    def down_dot(total, grads, count):
        def columns(i, carry):
            lanes = pl.ds(pl.multiple_of(i * 2 * LANES, 2 * LANES), 2 * LANES)
            term = dot_nn(grads, x_ref[:, lanes]) * norm_factor
            for l in range(2):
                for r in range(count):
                    total.terms[(i * 2 + l) * count + r] = (
                        term[r * ROWS:(r + 1) * ROWS, l * LANES:(l + 1) * LANES].astype(BF16))
            return carry

        lax.fori_loop(0, width // (2 * LANES), columns, 0)

    down_dot(first, rq_ref[...].astype(BF16), rank // ROWS)
    first.pair_start()
    returns[0].wait_recv()

    @pl.when(relay_in)
    def _():
        returns[1].wait_recv()

    owned = rkv[:, 0:rows] + r_in[0].astype(F32) + r_in[1].astype(F32)
    down_dot(later, owned.astype(BF16), 2 * rank // ROWS)
    later.pair_start()
    first.xy_start()
    later.xy_start()
    first.z_start()
    later.z_start()
    first.z_back()
    later.z_back()
    first.xy_back()
    later.xy_back()
    first.pair_back()
    later.pair_back()
    first.finish()

    def unpack_first(i, carry):
        lanes = pl.ds(pl.multiple_of(i * LANES, LANES), LANES)
        for r in range(rank // ROWS):
            gd_ref[r * ROWS:(r + 1) * ROWS, lanes] = first.out[i * (rank // ROWS) + r].astype(F32)
        return carry

    lax.fori_loop(0, width // LANES, unpack_first, 0)

    def unpack_up(h, carry):
        lanes = pl.ds(pl.multiple_of(h * LANES, LANES), LANES)
        for r in range(3 * rank // ROWS):
            gu_ref[r * ROWS:(r + 1) * ROWS, lanes] = (
                first.out[up_base + h * (3 * rank // ROWS) + r].astype(F32))
        return carry

    lax.fori_loop(0, heads, unpack_up, 0)
    later.finish()

    def unpack_later(i, carry):
        lanes = pl.ds(pl.multiple_of(i * LANES, LANES), LANES)
        for r in range(2 * rank // ROWS):
            gd_ref[rank + r * ROWS:rank + (r + 1) * ROWS, lanes] = (
                later.out[i * (2 * rank // ROWS) + r].astype(F32))
        return carry

    lax.fori_loop(0, width // LANES, unpack_later, 0)

    for g in range(2):
        low_copy(g).wait_send()

    @pl.when(relay_out)
    def _():
        for g in range(2):
            low_next(g).wait_send()

    def swap_sent(h, carry):
        for part in range(PARTS):
            swap(h, part).wait_send()
        return carry

    lax.fori_loop(0, heads, swap_sent, 0)

    @pl.when(relay_out)
    def _():
        lax.fori_loop(0, chunks, lambda c, carry: (relay(c).wait_send(), carry)[1], 0)

    returns[0].wait_send()

    @pl.when(relay_in)
    def _():
        returns[1].wait_send()

    lax.fori_loop(0, heads, lambda h, carry: (att_copy(h).wait(), carry)[1], 0)
    first.drain()
    later.drain()


def fused(nb, nt, norm_factor, step, window, hidden, modulation, down, up, fq, fk, fv, g):
    _, rows, width = hidden.shape
    across = fq.shape[2]
    heads = across // HEAD
    rank = up.shape[0] // 3
    dma = pltpu.SemaphoreType.DMA
    vmem = pltpu.VMEM
    smem = pl.BlockSpec(memory_space=pltpu.SMEM)
    anywhere = pl.BlockSpec(memory_space=pl.ANY)
    whole = pl.BlockSpec(memory_space=pltpu.VMEM)
    chunks = PARTS * heads
    blocks = 2 * (rows // TILE)
    first_tiles = (rank // ROWS) * (width // LANES) + (3 * rank // ROWS) * heads
    later_tiles = (2 * rank // ROWS) * (width // LANES)
    return pl.pallas_call(
        functools.partial(fused_kernel, nb, nt, rank, norm_factor),
        out_shape=[
            jax.ShapeDtypeStruct((1, rows, across), BF16),
            jax.ShapeDtypeStruct((3 * rank, width), F32),
            jax.ShapeDtypeStruct((3 * rank, across), F32),
        ],
        in_specs=[smem, smem] + [anywhere] * 8,
        out_specs=[anywhere, whole, whole],
        scratch_shapes=[
            vmem((rows, width), BF16), vmem(modulation.shape, F32), vmem((2, width), F32),
            vmem((LANES + 4 * rank, width), BF16), vmem(up.shape, BF16), vmem((heads, LANES, 3 * HEAD), BF16),
            vmem(fq.shape, BF16), vmem(fq.shape, BF16), vmem(fq.shape, BF16), vmem(fq.shape, BF16),
            vmem((heads, 2, rows, HEAD), BF16), vmem((heads, 2, rows, HEAD), BF16),
            vmem((2, rows // 4, LANES), BF16), vmem((4, rows // 4, LANES), BF16),
            vmem((rows, LANES), BF16), vmem((rows, LANES), BF16), vmem((rows, LANES), BF16),
            vmem((8, 3 * rows), F32), vmem((rows, HEAD), BF16),
            vmem((3 * rows, 2 * HEAD), BF16), vmem((3 * rows, 2 * HEAD), BF16),
            vmem((rows, 3 * rows), BF16), vmem((rows, 3 * rows), BF16),
            vmem((2 * rank, 3 * rows), F32), vmem((rank, rows), F32),
            vmem((2, 2 * rank, rows), BF16), vmem((2, 2 * rank, rows), BF16),
            vmem((heads, rows, HEAD), BF16),
            dma((blocks + 9,)), dma((heads,)),
            dma((chunks,)), dma((chunks,)), dma((chunks,)), dma((chunks,)),
            dma((4,)), dma((4,)), dma((2,)), dma((2,)),
        ] + sum_shapes(first_tiles, nb, nt) + sum_shapes(later_tiles, nb, nt),
        compiler_params=pltpu.CompilerParams(
            collective_id=0, has_side_effects=True, vmem_limit_bytes=60 << 20
        ),
        name="fused",
    )(step, window, hidden, modulation, down, up, fq, fk, fv, g)


def per_device(
    hidden,
    frozen_queries,
    frozen_keys,
    frozen_values,
    reward_output_gradient,
    truncation_step,
    modulation,
    adapter_down_weight,
    adapter_up_weight,
    window,
):
    slab_rows, width = hidden.shape[1:]
    across = frozen_queries.shape[2]
    rank = adapter_up_weight.shape[1]
    nb, nt = lax.axis_size("batch"), lax.axis_size("tiles")
    norm_factor = 1.0 / math.sqrt(hidden.shape[0] * nb * slab_rows * nt)
    down = adapter_down_weight.transpose(0, 2, 1).reshape(3 * rank, width)
    up = adapter_up_weight.reshape(3 * rank, across)
    attended, grad_down, grad_up = fused(
        nb, nt, norm_factor, truncation_step, window, hidden, modulation, down, up,
        frozen_queries, frozen_keys, frozen_values, reward_output_gradient,
    )
    grad_down = grad_down.reshape(3, rank, width).transpose(0, 2, 1)
    grad_up = grad_up.reshape(3, rank, across)
    return (attended, grad_down, grad_up)


def solution(mesh):
    placed = (
        P("batch", "tiles", None),
        P("batch", "tiles", None),
        P("batch", "tiles", None),
        P("batch", "tiles", None),
        P("batch", "tiles", None),
        P("batch"),
        P(),
        P(),
        P(),
        P("tiles", None),
    )
    return jax.shard_map(
        per_device,
        mesh=mesh,
        in_specs=placed,
        out_specs=(P("batch", "tiles", None), P(), P()),
        check_vma=False,
    )
```

```python
import functools
import math

import jax
import jax.numpy as jnp
from jax import lax
from jax.experimental import pallas as pl
from jax.experimental.pallas import tpu as pltpu
from jax.sharding import PartitionSpec as P

HEAD = 128
TILE = 128
GF = 2
GR = 2
LANES = 128
ROWS = 16
PARTS = 4
EARLY = 5
BF16 = jnp.bfloat16
F32 = jnp.float32


def dot_nt(a, b):
    return lax.dot_general(
        a, b, (((1,), (1,)), ((), ())), preferred_element_type=jnp.float32
    )


def dot_tn(a, b):
    return lax.dot_general(
        a, b, (((0,), (0,)), ((), ())), preferred_element_type=jnp.float32
    )


def dot_nn(a, b):
    return jnp.dot(a, b, preferred_element_type=jnp.float32)


def remote(src, dst, send, recv, peer):
    return pltpu.make_async_remote_copy(
        src_ref=src, dst_ref=dst, send_sem=send, recv_sem=recv,
        device_id=peer, device_id_type=pl.DeviceIdType.MESH,
    )


class Place:
    def __init__(self, nb, nt):
        self.nb, self.nt = nb, nt
        self.nx, self.nz = nb // 2, nt // 2
        self.nxy = 2 * self.nx
        b, t = lax.axis_index("batch"), lax.axis_index("tiles")
        self.b, self.t = b, t
        self.core, self.x = lax.rem(b, 2), b // 2
        self.y, self.z = lax.rem(t, 2), t // 2

    def core_peer(self):
        return {"batch": self.b + 1 - 2 * self.core}

    def xy_offset(self, d, sign):
        dx, dy = d // 2, d % 2
        x = lax.rem(self.x + sign * dx + self.nx, self.nx)
        return x, lax.rem(self.y + dy, 2)

    def xy_peer(self, d):
        x, y = self.xy_offset(d, 1)
        return {"batch": x * 2 + self.core, "tiles": self.z * 2 + y}

    def xy_index(self, d, sign):
        x, y = self.xy_offset(d, sign)
        return x * 2 + y

    def z_peer(self, e):
        return {"tiles": lax.rem(self.z + e, self.nz) * 2 + self.y}


def share_of(tiles, nb, nt):
    return -(-tiles // (nb * nt))


def split_tiles(rank, width, heads, nb, nt):
    one = (rank // ROWS) * (width // LANES)
    ups = (3 * rank // ROWS) * heads
    spare = min(ups, share_of(one, nb, nt) * nb * nt - one)
    return 2 * one + ups - spare, one + spare


def sum_shapes(tiles, nb, nt):
    share = share_of(tiles, nb, nt)
    nxy, nz = nb, nt // 2
    quarter = nz * share
    total = nb * nt * share
    dma = pltpu.SemaphoreType.DMA
    return [
        pltpu.VMEM((total, ROWS, LANES), BF16),
        pltpu.VMEM((total // 2, ROWS, LANES), BF16),
        pltpu.VMEM((nxy - 1, quarter, ROWS, LANES), BF16),
        pltpu.VMEM((nxy - 1, quarter, ROWS, LANES), BF16),
        pltpu.VMEM((quarter, ROWS, LANES), F32),
        pltpu.VMEM((nz - 1, share, ROWS, LANES), BF16),
        pltpu.VMEM((nz - 1, share, ROWS, LANES), BF16),
        dma((nxy,)), dma((nxy,)), dma((nxy - 1,)), dma((nxy - 1,)),
        dma((nz - 1,)), dma((nz - 1,)), dma((nz - 1,)), dma((nz - 1,)),
        dma((nxy - 1, nz)), dma((nxy - 1, nz)), dma((nxy, nz)), dma((nxy, nz)),
    ]


class Sum:
    def __init__(self, place, tiles, out, refs):
        self.place, self.tiles, self.out = place, tiles, out
        (self.terms, self.pair, self.part1, self.got1, self.acc, self.part2, self.got2,
         self.s0, self.r0, self.s1, self.r1, self.s2, self.r2, self.s3, self.r3,
         self.s4, self.r4, self.s5, self.r5) = refs
        self.share = share_of(tiles, place.nb, place.nt)
        self.quarter = place.nz * self.share
        self.half = place.nxy * self.quarter
        self.mine = place.core * self.half
        self.order = list(range(place.nxy - 1, -1, -1))
        self.sent = []

    def clear(self):
        pad = self.terms.shape[0] - self.tiles
        if pad:
            self.terms[self.tiles:] = jnp.zeros((pad, ROWS, LANES), BF16)

    def go(self, *args):
        copy = remote(*args)
        copy.start()
        self.sent.append(copy)
        return copy

    def pair_start(self):
        p = self.place
        other = (1 - p.core) * self.half
        self.c0 = {}
        for d in self.order:
            q = p.xy_index(d, 1) * self.quarter
            self.c0[d] = self.go(self.terms.at[pl.ds(other + q, self.quarter)],
                                 self.pair.at[pl.ds(q, self.quarter)],
                                 self.s0.at[d], self.r0.at[d], p.core_peer())

    def xy_start(self):
        p = self.place
        self.c1 = {}
        for d in self.order:
            q = p.xy_index(d, 1) * self.quarter
            self.c0[d].wait_recv()
            total = (self.terms[pl.ds(self.mine + q, self.quarter)].astype(F32)
                     + self.pair[pl.ds(q, self.quarter)].astype(F32))
            if d == 0:
                self.acc[...] = total
            else:
                self.part1[d - 1] = total.astype(BF16)
                self.c1[d] = self.go(self.part1.at[d - 1], self.got1.at[d - 1],
                                     self.s1.at[d - 1], self.r1.at[d - 1], p.xy_peer(d))

    def z_start(self):
        p = self.place
        for d in self.order:
            if d:
                self.c1[d].wait_recv()
        total = self.acc[...]
        for d in range(1, p.nxy):
            total = total + self.got1[d - 1].astype(F32)
        self.acc[...] = total
        self.c2 = []
        for e in range(1, p.nz):
            spot = lax.rem(p.z + e, p.nz) * self.share
            self.part2[e - 1] = self.acc[pl.ds(spot, self.share)].astype(BF16)
            self.c2.append(self.go(self.part2.at[e - 1], self.got2.at[e - 1],
                                   self.s2.at[e - 1], self.r2.at[e - 1], p.z_peer(e)))

    def spot(self, d, e):
        p = self.place
        plane = lax.rem(p.z - e + p.nz, p.nz) * self.share
        return self.out.at[pl.ds(self.mine + p.xy_index(d, -1) * self.quarter + plane, self.share)]

    def z_back(self):
        p = self.place
        total = self.acc[pl.ds(p.z * self.share, self.share)]
        for e in range(1, p.nz):
            self.c2[e - 1].wait_recv()
            total = total + self.got2[e - 1].astype(F32)
        mine = self.spot(0, 0)
        mine[...] = total.astype(BF16)
        self.c3 = [self.go(mine, mine, self.s3.at[e - 1], self.r3.at[e - 1], p.z_peer(e))
                   for e in range(1, p.nz)]

    def xy_back(self):
        p = self.place
        self.c4, self.c5 = {}, []
        for e in range(p.nz):
            if e:
                self.c3[e - 1].wait_recv()
            piece = self.spot(0, e)
            for d in self.order:
                if d:
                    self.c4[d, e] = self.go(piece, piece, self.s4.at[d - 1, e],
                                            self.r4.at[d - 1, e], p.xy_peer(d))
            self.c5.append(self.go(piece, piece, self.s5.at[0, e], self.r5.at[0, e],
                                   p.core_peer()))

    def pair_back(self):
        p = self.place
        for e in range(p.nz):
            for d in range(1, p.nxy):
                self.c4[d, e].wait_recv()
                piece = self.spot(d, e)
                self.c5.append(self.go(piece, piece, self.s5.at[d, e], self.r5.at[d, e],
                                       p.core_peer()))

    def finish(self):
        for copy in self.c5:
            copy.wait_recv()

    def drain(self):
        for copy in self.sent:
            copy.wait_send()


def fused_kernel(nb, nt, rank, norm_factor, step_ref, window_ref, hidden_hbm, mod_hbm, down_hbm, up_hbm,
                 fq_hbm, fk_hbm, fv_hbm, g_hbm,
                 att_hbm, first_out, later_out,
                 x_ref, mod_all, mod_ref, down_ref, up_ref, ups, fq_ref, fk_ref, fv_ref, g_ref,
                 swap_ref, relay_ref, low_pack, low_got, low_ref, low_swap, low_relay, bias_ref, q_ref, kl, vl,
                 probs_f, probs_s, grad_s, rkv, rq_ref, r_out, r_in, att_ref, up_terms,
                 load, att_sem, swap_send, swap_recv, relay_send, relay_recv,
                 low_send, low_recv, r_send, r_recv, *sums):
    place = Place(nb, nt)
    t_index, odd = place.t, place.y
    rows, across = fq_ref.shape[1:]
    heads = across // HEAD
    width = x_ref.shape[1]
    half = rows // 2
    chunks = PARTS * heads
    per = len(sums) // 2
    first_tiles, later_tiles = split_tiles(rank, width, heads, nb, nt)
    first = Sum(place, first_tiles, first_out, sums[:per])
    later = Sum(place, later_tiles, later_out, sums[per:])

    partner = {"tiles": t_index + 1 - 2 * odd}
    target = {"tiles": lax.rem(t_index + 2 - 4 * odd + nt, nt)}
    other = {"tiles": lax.rem(t_index - 1 + 2 * odd + nt, nt)}
    even = odd == 0
    relay_in = jnp.where(even, t_index >= 2, t_index < nt - 2)
    relay_out = jnp.where(even, t_index < nt - 2, t_index >= 2)

    blocks = rows // TILE
    block = TILE
    hidden_loads = [
        pltpu.make_async_copy(hidden_hbm.at[0, pl.ds(i * block, block)],
                              x_ref.at[pl.ds(i * block, block)], load.at[i])
        for i in range(blocks)
    ]
    others = [
        pltpu.make_async_copy(src, dst, load.at[blocks + i])
        for i, (src, dst) in enumerate((
            (mod_hbm, mod_all), (down_hbm, down_ref.at[pl.ds(0, 3 * rank)]),
            (up_hbm, up_ref),
            (fq_hbm, fq_ref), (fk_hbm, fk_ref), (fv_hbm, fv_ref), (g_hbm, g_ref)))
    ]

    barrier = pltpu.get_barrier_semaphore()
    greet = [place.core_peer(), other]
    greet += [place.xy_peer(d) for d in range(1, place.nxy)]
    greet += [place.z_peer(e) for e in range(1, place.nz)]
    for peer in greet:
        pl.semaphore_signal(barrier, inc=1, device_id=peer, device_id_type=pl.DeviceIdType.MESH)
    hidden_loads[0].start()
    for copy in others[:2]:
        copy.start()
    for copy in hidden_loads[1:]:
        copy.start()

    scale_root = 1.0 / math.sqrt(HEAD)
    scale_two = scale_root * math.log2(math.e)
    per_slab = GF * GR
    sides = (jnp.int32(9), 18 * (1 - odd), 18 * odd)
    for s, side in enumerate(sides):
        for t in range(per_slab):
            for u in range(per_slab):
                code = side + 3 * (u // GR - t // GR + 1) + u % GR - t % GR + 1
                value = jnp.where(window_ref[t, code] > 0, 0.0, -1e30).astype(F32)
                if s == 2:
                    value = jnp.where(relay_in, value, -1e30)
                spot = (s * per_slab + u) * TILE
                bias_ref[t:t + 1, spot:spot + TILE] = jnp.full((1, TILE), value, F32)

    pl.semaphore_wait(barrier, len(greet))

    def swap(h, part):
        src = (fk_hbm, fv_hbm)[part // 2]
        start = (part % 2) * half
        lanes = pl.ds(pl.multiple_of(h * HEAD, HEAD), HEAD)
        c = h * PARTS + part
        return remote(src.at[0, pl.ds(start, half), lanes],
                      swap_ref.at[h, part // 2, pl.ds(start, half)],
                      swap_send.at[c], swap_recv.at[c], partner)

    def chunk(ref, c):
        return ref.at[c // PARTS, lax.rem(c, PARTS) // 2, pl.ds(lax.rem(c, 2) * half, half)]

    def relay(c):
        return remote(chunk(swap_ref, c), chunk(relay_ref, c), relay_send.at[c], relay_recv.at[c],
                      target)

    def pump(c):
        remote(chunk(swap_ref, c), chunk(swap_ref, c), swap_send.at[c], swap_recv.at[c],
               partner).wait_recv()

        @pl.when(relay_out)
        def _():
            relay(c).start()

    for c in range(EARLY):
        swap(c // PARTS, c % PARTS).start()

    @pl.when(jnp.logical_not(relay_in))
    def _():
        low_relay[...] = jnp.zeros_like(low_relay)

        def clear(h, carry):
            relay_ref[h] = jnp.zeros(relay_ref.shape[1:], BF16)
            return carry

        lax.fori_loop(0, heads, clear, 0)
        for j in range(2):
            r_in[2 * j + 1] = jnp.zeros(r_in.shape[1:], BF16)

    first.clear()
    later.clear()
    rq_ref[...] = jnp.zeros_like(rq_ref)
    rkv[...] = jnp.zeros_like(rkv)
    ups[...] = jnp.zeros_like(ups)
    down_ref[3 * rank:LANES] = jnp.zeros((LANES - 3 * rank, width), BF16)

    for copy in others[:2]:
        copy.wait()
    mod_ref[...] = mod_all[step_ref[0]]
    row = lax.broadcasted_iota(jnp.int32, (LANES, LANES), 0)
    lane = lax.broadcasted_iota(jnp.int32, (LANES, LANES), 1)
    wide = 2 * rank

    def low_copy(g):
        return remote(low_pack.at[g], low_got.at[g], low_send.at[g], low_recv.at[g], partner)

    def low_next(g):
        return remote(low_got.at[g], low_got.at[2 + g], low_send.at[2 + g], low_recv.at[2 + g],
                      target)

    def one_hot(pick):
        return jnp.where(pick, 1.0, 0.0).astype(BF16)

    def pack_low(g):
        total = jnp.zeros((rows // 4, LANES), F32)
        for part in range(2):
            pick = jnp.logical_and(lane // wide == part, row - rank == lane - part * wide)
            start = (2 * g + part) * (rows // 4)
            total = total + dot_nn(low_ref[start:start + rows // 4, :], one_hot(pick))
        low_pack[g] = total.astype(BF16)
        low_copy(g).start()

    def modulate(i, carry):
        span = pl.ds(pl.multiple_of(i * block, block), block)
        pltpu.make_async_copy(hidden_hbm.at[0, span], x_ref.at[span], load.at[i]).wait()
        x = x_ref[span, :].astype(F32)
        mean = jnp.sum(x, axis=1, keepdims=True) * (1.0 / width)
        centred = x - mean
        variance = jnp.sum(centred * centred, axis=1, keepdims=True) * (1.0 / width)
        normed = centred * lax.rsqrt(variance + 1e-06)
        x_low = (normed * (1.0 + mod_ref[1:2, :]) + mod_ref[0:1, :]).astype(BF16)
        x_ref[span, :] = x_low
        low_ref[span, :] = dot_nt(x_low, down_ref[...]).astype(BF16)
        return carry

    half_blocks = blocks // 2
    lax.fori_loop(0, half_blocks, modulate, 0)
    pack_low(0)
    lax.fori_loop(half_blocks, blocks - 1, modulate, 0)
    pump(0)
    lax.fori_loop(blocks - 1, blocks, modulate, 0)
    pack_low(1)
    for c in range(EARLY, 2 * PARTS):
        swap(c // PARTS, c % PARTS).start()

    def send_rest(h, carry):
        for part in range(PARTS):
            swap(h, part).start()
        return carry

    lax.fori_loop(2, heads, send_rest, 0)
    for copy in others[2:]:
        copy.start()
    pump(1)
    for copy in others[2:]:
        copy.wait()

    def build(h, carry):
        lanes = pl.ds(pl.multiple_of(h * HEAD, HEAD), HEAD)
        for j in range(3):
            ups[h, j * rank:(j + 1) * rank, j * HEAD:(j + 1) * HEAD] = (
                up_ref[j * rank:(j + 1) * rank, lanes])
        return carry

    lax.fori_loop(0, heads, build, 0)
    pump(2)
    pump(3)
    for g in range(2):
        low_copy(g).wait_recv()

        @pl.when(relay_out)
        def _(g=g):
            low_next(g).start()

    inside = jnp.logical_and(lane >= rank, lane < 3 * rank)

    def unpack_low(s, dst):
        quarter = rows // 4
        for part in range(2):
            pick = jnp.logical_and(inside, row == lane - rank + part * wide)
            select = one_hot(pick)
            for g in range(2):
                start = (2 * g + part) * quarter
                dst[start:start + quarter, :] = dot_nn(low_got[2 * s + g], select).astype(BF16)

    unpack_low(0, low_swap)

    @pl.when(relay_in)
    def _():
        for g in range(2):
            low_next(g).wait_recv()
        unpack_low(1, low_relay)

    def value_return(s):
        return remote(r_out.at[s], r_in.at[s], r_send.at[s], r_recv.at[s], (partner, other)[s])

    def key_return(s):
        return remote(r_out.at[2 + s], r_in.at[2 + s], r_send.at[2 + s], r_recv.at[2 + s],
                      (partner, other)[s])

    def send_back(ready, start):
        base = 0 if ready is value_return else 2
        for s in range(2):
            r_out[base + s] = rkv[start:start + rank, (s + 1) * rows:(s + 2) * rows].astype(BF16)
        ready(0).start()

        @pl.when(relay_in)
        def _():
            ready(1).start()

    def take_back(ready, start):
        base = 0 if ready is value_return else 2
        ready(0).wait_recv()

        @pl.when(relay_in)
        def _():
            ready(1).wait_recv()

        return (rkv[start:start + rank, 0:rows] + r_in[base].astype(F32)
                + r_in[base + 1].astype(F32)).astype(BF16)

    for s, low in enumerate((low_ref, low_swap, low_relay)):
        kl[s * rows:(s + 1) * rows, HEAD:] = low[...]
        vl[s * rows:(s + 1) * rows, HEAD:] = low[...]


    def att_copy(h):
        lanes = pl.ds(pl.multiple_of(h * HEAD, HEAD), HEAD)
        return pltpu.make_async_copy(att_ref.at[h], att_hbm.at[0, :, lanes], att_sem.at[h])

    def pump_next(h, part):
        @pl.when(h + 1 < heads)
        def _():
            pump((h + 1) * PARTS + part)

    def arrive(h, part):
        @pl.when(relay_in)
        def _():
            for i in range(2):
                relay(h * PARTS + 2 * part + i).wait_recv()

    def one_head(h, carry):
        lanes = pl.ds(pl.multiple_of(h * HEAD, HEAD), HEAD)
        own = dot_nn(low_ref[...], ups[h])
        q_ref[...] = (fq_ref[0, :, lanes].astype(F32) + own[:, 0:HEAD]).astype(BF16)
        kl[0:rows, 0:HEAD] = (fk_ref[0, :, lanes].astype(F32) + own[:, HEAD:2 * HEAD]).astype(BF16)
        vl[0:rows, 0:HEAD] = (fv_ref[0, :, lanes].astype(F32) + own[:, 2 * HEAD:]).astype(BF16)
        g_up = dot_nt(up_ref[2 * rank:3 * rank, lanes], g_ref[0, :, lanes]).astype(BF16)
        q_up = dot_nt(up_ref[rank:2 * rank, lanes], q_ref[...]).astype(BF16)

        def rebuild(dst, part):
            for s, (low, got) in enumerate(((low_swap, swap_ref), (low_relay, relay_ref))):
                add = dot_nn(low[...], ups[h, :, (part + 1) * HEAD:(part + 2) * HEAD])
                dst[(s + 1) * rows:(s + 2) * rows, 0:HEAD] = (
                    got[h, part].astype(F32) + add).astype(BF16)

        arrive(h, 0)
        rebuild(kl, 0)
        for t in range(rows // TILE):
            span = slice(t * TILE, (t + 1) * TILE)
            scores = dot_nt(q_ref[span, :], kl[:, 0:HEAD]) * scale_two + bias_ref[t:t + 1, :]
            top = jnp.max(scores, axis=1, keepdims=True)
            weights = jnp.exp2(scores - top)
            inverse = 1.0 / jnp.sum(weights, axis=1, keepdims=True)
            probs = weights * inverse
            probs_f[span, :] = probs
            probs_s[span, :] = probs.astype(BF16)
            if t == rows // TILE // 2:
                pump_next(h, 0)
        rkv[rank:2 * rank, :] += dot_nn(g_up, probs_s[...])

        @pl.when(h == heads - 1)
        def _():
            send_back(value_return, rank)

        pump_next(h, 1)
        arrive(h, 1)
        rebuild(vl, 1)
        for t in range(rows // TILE):
            span = slice(t * TILE, (t + 1) * TILE)
            prob_grad = dot_nt(g_ref[0, span, lanes], vl[:, 0:HEAD])
            probs = probs_f[span, :]
            centre = jnp.sum(probs * prob_grad, axis=1, keepdims=True)
            grad_s[span, :] = (probs * (prob_grad - centre) * scale_root).astype(BF16)
            if t == rows // TILE // 2:
                pump_next(h, 2)
        rkv[0:rank, :] += dot_nn(q_up, grad_s[...])

        @pl.when(h == heads - 1)
        def _():
            send_back(key_return, 0)

        q_all = q_ref[...]
        g_all = g_ref[0, :, lanes]
        dq = dot_nn(grad_s[...], kl[...])
        dq_low = dq[:, 0:HEAD].astype(BF16)
        low_k = dq[:, HEAD:].astype(BF16)
        rq_ref[...] += dot_nt(up_ref[0:rank, lanes], dq_low)
        att = dot_nn(probs_s[...], vl[...])
        att_ref[h] = att[:, 0:HEAD].astype(BF16)
        att_copy(h).start()
        low_v = att[:, HEAD:].astype(BF16)
        ups_terms = (dot_tn(low_ref[...], dq_low), dot_tn(low_k, q_all), dot_tn(low_v, g_all))
        for j, term in enumerate(ups_terms):
            for r in range(rank // ROWS):
                start = j * rank + r * ROWS
                spot = h * (3 * rank // ROWS) + start // ROWS
                up_terms[spot] = (term[start:start + ROWS] * norm_factor).astype(BF16)
        pump_next(h, 3)
        return carry

    lax.fori_loop(0, heads, one_head, 0)

    def down_dot(total, grads, count):
        def columns(i, carry):
            lanes = pl.ds(pl.multiple_of(i * 2 * LANES, 2 * LANES), 2 * LANES)
            term = dot_nn(grads, x_ref[:, lanes]) * norm_factor
            for l in range(2):
                for r in range(count):
                    total.terms[(i * 2 + l) * count + r] = (
                        term[r * ROWS:(r + 1) * ROWS, l * LANES:(l + 1) * LANES].astype(BF16))
            return carry

        lax.fori_loop(0, width // (2 * LANES), columns, 0)

    one = (rank // ROWS) * (width // LANES)
    kept = first_tiles - 2 * one
    if kept:
        first.terms[2 * one:first_tiles] = up_terms[0:kept]
    if later_tiles > one:
        later.terms[one:later_tiles] = up_terms[kept:]
    grads = jnp.concatenate([rq_ref[...].astype(BF16), take_back(value_return, rank)], axis=0)
    down_dot(first, grads, 2 * rank // ROWS)
    first.pair_start()
    grads = take_back(key_return, 0)
    down_dot(later, grads, rank // ROWS)
    later.pair_start()
    first.xy_start()
    later.xy_start()
    first.z_start()
    later.z_start()
    first.z_back()
    later.z_back()
    first.xy_back()
    later.xy_back()
    first.pair_back()
    later.pair_back()
    first.finish()
    later.finish()

    for g in range(2):
        low_copy(g).wait_send()

    @pl.when(relay_out)
    def _():
        for g in range(2):
            low_next(g).wait_send()

    def swap_sent(h, carry):
        for part in range(PARTS):
            swap(h, part).wait_send()
        return carry

    lax.fori_loop(0, heads, swap_sent, 0)

    @pl.when(relay_out)
    def _():
        lax.fori_loop(0, chunks, lambda c, carry: (relay(c).wait_send(), carry)[1], 0)

    for ready in (value_return, key_return):
        ready(0).wait_send()

    @pl.when(relay_in)
    def _():
        for ready in (value_return, key_return):
            ready(1).wait_send()

    lax.fori_loop(0, heads, lambda h, carry: (att_copy(h).wait(), carry)[1], 0)
    first.drain()
    later.drain()


def fused(nb, nt, norm_factor, step, window, hidden, modulation, down, up, fq, fk, fv, g):
    _, rows, width = hidden.shape
    across = fq.shape[2]
    heads = across // HEAD
    rank = up.shape[0] // 3
    dma = pltpu.SemaphoreType.DMA
    vmem = pltpu.VMEM
    smem = pl.BlockSpec(memory_space=pltpu.SMEM)
    anywhere = pl.BlockSpec(memory_space=pl.ANY)
    whole = pl.BlockSpec(memory_space=pltpu.VMEM)
    chunks = PARTS * heads
    blocks = rows // TILE
    first_tiles, later_tiles = split_tiles(rank, width, heads, nb, nt)
    totals = [share_of(tiles, nb, nt) * nb * nt for tiles in (first_tiles, later_tiles)]
    return pl.pallas_call(
        functools.partial(fused_kernel, nb, nt, rank, norm_factor),
        out_shape=[
            jax.ShapeDtypeStruct((1, rows, across), BF16),
            jax.ShapeDtypeStruct((totals[0], ROWS, LANES), BF16),
            jax.ShapeDtypeStruct((totals[1], ROWS, LANES), BF16),
        ],
        in_specs=[smem, smem] + [anywhere] * 8,
        out_specs=[anywhere, whole, whole],
        scratch_shapes=[
            vmem((rows, width), BF16), vmem(modulation.shape, F32), vmem((2, width), F32),
            vmem((LANES, width), BF16), vmem(up.shape, BF16), vmem((heads, LANES, 3 * HEAD), BF16),
            vmem(fq.shape, BF16), vmem(fq.shape, BF16), vmem(fq.shape, BF16), vmem(fq.shape, BF16),
            vmem((heads, 2, rows, HEAD), BF16), vmem((heads, 2, rows, HEAD), BF16),
            vmem((2, rows // 4, LANES), BF16), vmem((4, rows // 4, LANES), BF16),
            vmem((rows, LANES), BF16), vmem((rows, LANES), BF16), vmem((rows, LANES), BF16),
            vmem((8, 3 * rows), F32), vmem((rows, HEAD), BF16),
            vmem((3 * rows, 2 * HEAD), BF16), vmem((3 * rows, 2 * HEAD), BF16),
            vmem((rows, 3 * rows), F32),
            vmem((rows, 3 * rows), BF16), vmem((rows, 3 * rows), BF16),
            vmem((2 * rank, 3 * rows), F32), vmem((rank, rows), F32),
            vmem((4, rank, rows), BF16), vmem((4, rank, rows), BF16),
            vmem((heads, rows, HEAD), BF16), vmem((heads * (3 * rank // ROWS), ROWS, LANES), BF16),
            dma((blocks + 7,)), dma((heads,)),
            dma((chunks,)), dma((chunks,)), dma((chunks,)), dma((chunks,)),
            dma((4,)), dma((4,)), dma((4,)), dma((4,)),
        ] + sum_shapes(first_tiles, nb, nt) + sum_shapes(later_tiles, nb, nt),
        compiler_params=pltpu.CompilerParams(
            collective_id=0, has_side_effects=True, vmem_limit_bytes=60 << 20
        ),
        name="fused",
    )(step, window, hidden, modulation, down, up, fq, fk, fv, g)


def place_kernel(rank, att_hbm, first_hbm, later_hbm, att_out, down_out, up_out,
                 att_ref, first_ref, later_ref, down_ref, up_ref, load, store):
    rows, across = att_ref.shape[1:]
    heads = across // HEAD
    width = down_ref.shape[1]
    one = (rank // ROWS) * (width // LANES)
    parts = 4
    cut = rows // parts
    takes = [pltpu.make_async_copy(first_hbm, first_ref, load.at[0]),
             pltpu.make_async_copy(later_hbm, later_ref, load.at[1])]
    moves = [(pltpu.make_async_copy(att_hbm.at[:, pl.ds(i * cut, cut)],
                                    att_ref.at[:, pl.ds(i * cut, cut)], load.at[2 + i]),
              pltpu.make_async_copy(att_ref.at[:, pl.ds(i * cut, cut)],
                                    att_out.at[:, pl.ds(i * cut, cut)], store.at[2 + i]))
             for i in range(parts)]
    for copy in takes:
        copy.start()
    for copy, _ in moves:
        copy.start()
    for copy in takes:
        copy.wait()
    step = rank // ROWS
    for l in range(width // LANES):
        lanes = slice(l * LANES, (l + 1) * LANES)
        for r in range(step):
            spots = (first_ref[l * 2 * step + r], later_ref[l * step + r],
                     first_ref[l * 2 * step + step + r])
            for j, tile in enumerate(spots):
                down_ref[j * rank + r * ROWS:j * rank + (r + 1) * ROWS, lanes] = tile.astype(F32)
    down_store = pltpu.make_async_copy(down_ref, down_out, store.at[0])
    down_store.start()
    spare = min(3 * step * heads, later_ref.shape[0] - one)
    kept = 3 * step * heads - spare
    for h in range(heads):
        lanes = slice(h * HEAD, (h + 1) * HEAD)
        for r in range(3 * step):
            k = h * 3 * step + r
            tile = first_ref[2 * one + k] if k < kept else later_ref[one + k - kept]
            up_ref[r * ROWS:(r + 1) * ROWS, lanes] = tile.astype(F32)
    up_store = pltpu.make_async_copy(up_ref, up_out, store.at[1])
    up_store.start()
    for copy, then in moves:
        copy.wait()
        then.start()
    for _, then in moves:
        then.wait()
    down_store.wait()
    up_store.wait()


def put_in_place(rank, width, attended, first, later):
    across = attended.shape[2]
    vmem, dma = pltpu.VMEM, pltpu.SemaphoreType.DMA
    anywhere = pl.BlockSpec(memory_space=pl.ANY)
    return pl.pallas_call(
        functools.partial(place_kernel, rank),
        out_shape=[
            jax.ShapeDtypeStruct(attended.shape, BF16),
            jax.ShapeDtypeStruct((3 * rank, width), F32),
            jax.ShapeDtypeStruct((3 * rank, across), F32),
        ],
        in_specs=[anywhere] * 3,
        out_specs=[anywhere] * 3,
        scratch_shapes=[
            vmem(attended.shape, BF16), vmem(first.shape, BF16), vmem(later.shape, BF16),
            vmem((3 * rank, width), F32), vmem((3 * rank, across), F32), dma((6,)), dma((6,)),
        ],
        name="place",
    )(attended, first, later)


def per_device(
    hidden,
    frozen_queries,
    frozen_keys,
    frozen_values,
    reward_output_gradient,
    truncation_step,
    modulation,
    adapter_down_weight,
    adapter_up_weight,
    window,
):
    slab_rows, width = hidden.shape[1:]
    across = frozen_queries.shape[2]
    rank = adapter_up_weight.shape[1]
    nb, nt = lax.axis_size("batch"), lax.axis_size("tiles")
    norm_factor = 1.0 / math.sqrt(hidden.shape[0] * nb * slab_rows * nt)
    down = adapter_down_weight.transpose(0, 2, 1).reshape(3 * rank, width)
    up = adapter_up_weight.reshape(3 * rank, across)
    attended, first, later = fused(
        nb, nt, norm_factor, truncation_step, window, hidden, modulation, down, up,
        frozen_queries, frozen_keys, frozen_values, reward_output_gradient,
    )
    attended, grad_down, grad_up = put_in_place(rank, width, attended, first, later)
    grad_down = grad_down.reshape(3, rank, width).transpose(0, 2, 1)
    grad_up = grad_up.reshape(3, rank, across)
    return (attended, grad_down, grad_up)


def solution(mesh):
    placed = (
        P("batch", "tiles", None),
        P("batch", "tiles", None),
        P("batch", "tiles", None),
        P("batch", "tiles", None),
        P("batch", "tiles", None),
        P("batch"),
        P(),
        P(),
        P(),
        P("tiles", None),
    )
    return jax.shard_map(
        per_device,
        mesh=mesh,
        in_specs=placed,
        out_specs=(P("batch", "tiles", None), P(), P()),
        check_vma=False,
    )
```

```python
import functools
import math

import jax
import jax.numpy as jnp
from jax import lax
from jax.experimental import pallas as pl
from jax.experimental.pallas import tpu as pltpu
from jax.sharding import PartitionSpec as P

HEAD = 128
TILE = 128
GF = 2
GR = 2
LANES = 128
ROWS = 16
PARTS = 4
EARLY = 4
AHEAD = 7
BF16 = jnp.bfloat16
F32 = jnp.float32


def dot_nt(a, b):
    return lax.dot_general(
        a, b, (((1,), (1,)), ((), ())), preferred_element_type=jnp.float32
    )


def dot_tn(a, b):
    return lax.dot_general(
        a, b, (((0,), (0,)), ((), ())), preferred_element_type=jnp.float32
    )


def dot_nn(a, b):
    return jnp.dot(a, b, preferred_element_type=jnp.float32)


def remote(src, dst, send, recv, peer):
    return pltpu.make_async_remote_copy(
        src_ref=src, dst_ref=dst, send_sem=send, recv_sem=recv,
        device_id=peer, device_id_type=pl.DeviceIdType.MESH,
    )


class Place:
    def __init__(self, nb, nt):
        self.nb, self.nt = nb, nt
        self.nx, self.nz = nb // 2, nt // 2
        self.nxy = 2 * self.nx
        b, t = lax.axis_index("batch"), lax.axis_index("tiles")
        self.b, self.t = b, t
        self.core, self.x = lax.rem(b, 2), b // 2
        self.y, self.z = lax.rem(t, 2), t // 2

    def core_peer(self):
        return {"batch": self.b + 1 - 2 * self.core}

    def xy_offset(self, d, sign):
        dx, dy = d // 2, d % 2
        x = lax.rem(self.x + sign * dx + self.nx, self.nx)
        return x, lax.rem(self.y + dy, 2)

    def xy_peer(self, d):
        x, y = self.xy_offset(d, 1)
        return {"batch": x * 2 + self.core, "tiles": self.z * 2 + y}

    def xy_index(self, d, sign):
        x, y = self.xy_offset(d, sign)
        return x * 2 + y

    def z_peer(self, e):
        return {"tiles": lax.rem(self.z + e, self.nz) * 2 + self.y}


def share_of(tiles, nb, nt):
    return -(-tiles // (nb * nt))


def split_tiles(rank, width, heads, nb, nt):
    one = (rank // ROWS) * (width // LANES)
    ups = (3 * rank // ROWS) * heads
    spare = min(ups, share_of(one, nb, nt) * nb * nt - one)
    return 2 * one + ups - spare, one + spare


def sum_shapes(tiles, nb, nt):
    share = share_of(tiles, nb, nt)
    nxy, nz = nb, nt // 2
    quarter = nz * share
    total = nb * nt * share
    dma = pltpu.SemaphoreType.DMA
    return [
        pltpu.VMEM((total, ROWS, LANES), BF16),
        pltpu.VMEM((total // 2, ROWS, LANES), BF16),
        pltpu.VMEM((nxy - 1, quarter, ROWS, LANES), BF16),
        pltpu.VMEM((nxy - 1, quarter, ROWS, LANES), BF16),
        pltpu.VMEM((quarter, ROWS, LANES), F32),
        pltpu.VMEM((nz - 1, share, ROWS, LANES), BF16),
        pltpu.VMEM((nz - 1, share, ROWS, LANES), BF16),
        dma((nxy,)), dma((nxy,)), dma((nxy - 1,)), dma((nxy - 1,)),
        dma((nz - 1,)), dma((nz - 1,)), dma((nz - 1,)), dma((nz - 1,)),
        dma((nxy - 1, nz)), dma((nxy - 1, nz)), dma((nxy, nz)), dma((nxy, nz)),
    ]


class Sum:
    def __init__(self, place, tiles, out, refs):
        self.place, self.tiles, self.out = place, tiles, out
        (self.terms, self.pair, self.part1, self.got1, self.acc, self.part2, self.got2,
         self.s0, self.r0, self.s1, self.r1, self.s2, self.r2, self.s3, self.r3,
         self.s4, self.r4, self.s5, self.r5) = refs
        self.share = share_of(tiles, place.nb, place.nt)
        self.quarter = place.nz * self.share
        self.half = place.nxy * self.quarter
        self.mine = place.core * self.half
        self.order = list(range(place.nxy - 1, -1, -1))
        self.sent = []

    def clear(self):
        pad = self.terms.shape[0] - self.tiles
        if pad:
            self.terms[self.tiles:] = jnp.zeros((pad, ROWS, LANES), BF16)

    def go(self, *args):
        copy = remote(*args)
        copy.start()
        self.sent.append(copy)
        return copy

    def pair_start(self):
        p = self.place
        other = (1 - p.core) * self.half
        self.c0 = {}
        for d in self.order:
            q = p.xy_index(d, 1) * self.quarter
            self.c0[d] = self.go(self.terms.at[pl.ds(other + q, self.quarter)],
                                 self.pair.at[pl.ds(q, self.quarter)],
                                 self.s0.at[d], self.r0.at[d], p.core_peer())

    def xy_start(self):
        p = self.place
        self.c1 = {}
        for d in self.order:
            q = p.xy_index(d, 1) * self.quarter
            self.c0[d].wait_recv()
            total = (self.terms[pl.ds(self.mine + q, self.quarter)].astype(F32)
                     + self.pair[pl.ds(q, self.quarter)].astype(F32))
            if d == 0:
                self.acc[...] = total
            else:
                self.part1[d - 1] = total.astype(BF16)
                self.c1[d] = self.go(self.part1.at[d - 1], self.got1.at[d - 1],
                                     self.s1.at[d - 1], self.r1.at[d - 1], p.xy_peer(d))

    def z_start(self):
        p = self.place
        for d in self.order:
            if d:
                self.c1[d].wait_recv()
        total = self.acc[...]
        for d in range(1, p.nxy):
            total = total + self.got1[d - 1].astype(F32)
        self.acc[...] = total
        self.c2 = []
        for e in range(1, p.nz):
            spot = lax.rem(p.z + e, p.nz) * self.share
            self.part2[e - 1] = self.acc[pl.ds(spot, self.share)].astype(BF16)
            self.c2.append(self.go(self.part2.at[e - 1], self.got2.at[e - 1],
                                   self.s2.at[e - 1], self.r2.at[e - 1], p.z_peer(e)))

    def spot(self, d, e):
        p = self.place
        plane = lax.rem(p.z - e + p.nz, p.nz) * self.share
        return self.out.at[pl.ds(self.mine + p.xy_index(d, -1) * self.quarter + plane, self.share)]

    def z_back(self):
        p = self.place
        total = self.acc[pl.ds(p.z * self.share, self.share)]
        for e in range(1, p.nz):
            self.c2[e - 1].wait_recv()
            total = total + self.got2[e - 1].astype(F32)
        mine = self.spot(0, 0)
        mine[...] = total.astype(BF16)
        self.c3 = [self.go(mine, mine, self.s3.at[e - 1], self.r3.at[e - 1], p.z_peer(e))
                   for e in range(1, p.nz)]

    def xy_back(self):
        p = self.place
        self.c4, self.c5 = {}, []
        for e in range(p.nz):
            if e:
                self.c3[e - 1].wait_recv()
            piece = self.spot(0, e)
            for d in self.order:
                if d:
                    self.c4[d, e] = self.go(piece, piece, self.s4.at[d - 1, e],
                                            self.r4.at[d - 1, e], p.xy_peer(d))
            self.c5.append(self.go(piece, piece, self.s5.at[0, e], self.r5.at[0, e],
                                   p.core_peer()))

    def pair_back(self):
        p = self.place
        for e in range(p.nz):
            for d in range(1, p.nxy):
                self.c4[d, e].wait_recv()
                piece = self.spot(d, e)
                self.c5.append(self.go(piece, piece, self.s5.at[d, e], self.r5.at[d, e],
                                       p.core_peer()))

    def finish(self):
        for copy in self.c5:
            copy.wait_recv()

    def drain(self):
        for copy in self.sent:
            copy.wait_send()


def fused_kernel(nb, nt, rank, norm_factor, step_ref, window_ref, hidden_hbm, mod_hbm, down_hbm, up_hbm,
                 fq_hbm, fk_hbm, fv_hbm, g_hbm,
                 att_hbm, first_out, later_out,
                 x_ref, mod_all, mod_ref, down_ref, up_ref, ups, fq_ref, fk_ref, fv_ref, g_ref,
                 swap_ref, relay_ref, low_pack, low_got, low_ref, low_swap, low_relay, bias_ref, q_ref, kl, vl,
                 probs_s, grad_s, rkv, rq_ref, r_out, r_in, att_ref, up_terms,
                 load, att_sem, swap_send, swap_recv, relay_send, relay_recv,
                 low_send, low_recv, r_send, r_recv, *sums):
    place = Place(nb, nt)
    t_index, odd = place.t, place.y
    rows, across = fq_ref.shape[1:]
    heads = across // HEAD
    width = x_ref.shape[1]
    half = rows // 2
    chunks = PARTS * heads
    per = len(sums) // 2
    first_tiles, later_tiles = split_tiles(rank, width, heads, nb, nt)
    first = Sum(place, first_tiles, first_out, sums[:per])
    later = Sum(place, later_tiles, later_out, sums[per:])

    partner = {"tiles": t_index + 1 - 2 * odd}
    target = {"tiles": lax.rem(t_index + 2 - 4 * odd + nt, nt)}
    other = {"tiles": lax.rem(t_index - 1 + 2 * odd + nt, nt)}
    even = odd == 0
    relay_in = jnp.where(even, t_index >= 2, t_index < nt - 2)
    relay_out = jnp.where(even, t_index < nt - 2, t_index >= 2)

    blocks = rows // TILE
    block = TILE
    hidden_loads = [
        pltpu.make_async_copy(hidden_hbm.at[0, pl.ds(i * block, block)],
                              x_ref.at[pl.ds(i * block, block)], load.at[i])
        for i in range(blocks)
    ]
    others = [
        pltpu.make_async_copy(src, dst, load.at[blocks + i])
        for i, (src, dst) in enumerate((
            (mod_hbm, mod_all), (down_hbm, down_ref.at[pl.ds(0, 3 * rank)]),
            (up_hbm, up_ref),
            (fq_hbm, fq_ref), (fk_hbm, fk_ref), (fv_hbm, fv_ref), (g_hbm, g_ref)))
    ]

    barrier = pltpu.get_barrier_semaphore()
    greet = [place.core_peer(), other]
    greet += [place.xy_peer(d) for d in range(1, place.nxy)]
    greet += [place.z_peer(e) for e in range(1, place.nz)]
    for peer in greet:
        pl.semaphore_signal(barrier, inc=1, device_id=peer, device_id_type=pl.DeviceIdType.MESH)
    hidden_loads[0].start()
    for copy in others[:2]:
        copy.start()
    for copy in hidden_loads[1:]:
        copy.start()

    scale_root = 1.0 / math.sqrt(HEAD)
    scale_two = scale_root * math.log2(math.e)
    per_slab = GF * GR
    sides = (jnp.int32(9), 18 * (1 - odd), 18 * odd)
    for s, side in enumerate(sides):
        for t in range(per_slab):
            for u in range(per_slab):
                code = side + 3 * (u // GR - t // GR + 1) + u % GR - t % GR + 1
                value = jnp.where(window_ref[t, code] > 0, 0.0, -1e30).astype(F32)
                if s == 2:
                    value = jnp.where(relay_in, value, -1e30)
                spot = (s * per_slab + u) * TILE
                bias_ref[t:t + 1, spot:spot + TILE] = jnp.full((1, TILE), value, F32)

    pl.semaphore_wait(barrier, len(greet))

    def swap(h, part):
        src = (fk_hbm, fv_hbm)[part // 2]
        start = (part % 2) * half
        lanes = pl.ds(pl.multiple_of(h * HEAD, HEAD), HEAD)
        c = h * PARTS + part
        return remote(src.at[0, pl.ds(start, half), lanes],
                      swap_ref.at[h, part // 2, pl.ds(start, half)],
                      swap_send.at[c], swap_recv.at[c], partner)

    def chunk(ref, c):
        return ref.at[c // PARTS, lax.rem(c, PARTS) // 2, pl.ds(lax.rem(c, 2) * half, half)]

    def relay(c):
        return remote(chunk(swap_ref, c), chunk(relay_ref, c), relay_send.at[c], relay_recv.at[c],
                      target)

    def pump(c):
        remote(chunk(swap_ref, c), chunk(swap_ref, c), swap_send.at[c], swap_recv.at[c],
               partner).wait_recv()

        @pl.when(relay_out)
        def _():
            relay(c).start()

    for c in range(EARLY):
        swap(c // PARTS, c % PARTS).start()

    @pl.when(jnp.logical_not(relay_in))
    def _():
        low_relay[...] = jnp.zeros_like(low_relay)

        def clear(h, carry):
            relay_ref[h] = jnp.zeros(relay_ref.shape[1:], BF16)
            return carry

        lax.fori_loop(0, heads, clear, 0)
        for j in range(2):
            r_in[2 * j + 1] = jnp.zeros(r_in.shape[1:], BF16)

    first.clear()
    later.clear()
    rq_ref[...] = jnp.zeros_like(rq_ref)
    rkv[...] = jnp.zeros_like(rkv)
    ups[...] = jnp.zeros_like(ups)
    down_ref[3 * rank:LANES] = jnp.zeros((LANES - 3 * rank, width), BF16)

    for copy in others[:2]:
        copy.wait()
    mod_ref[...] = mod_all[step_ref[0]]
    row = lax.broadcasted_iota(jnp.int32, (LANES, LANES), 0)
    lane = lax.broadcasted_iota(jnp.int32, (LANES, LANES), 1)
    wide = 2 * rank

    def low_copy(g):
        return remote(low_pack.at[g], low_got.at[g], low_send.at[g], low_recv.at[g], partner)

    def low_next(g):
        return remote(low_got.at[g], low_got.at[2 + g], low_send.at[2 + g], low_recv.at[2 + g],
                      target)

    def one_hot(pick):
        return jnp.where(pick, 1.0, 0.0).astype(BF16)

    def pack_low(g):
        total = jnp.zeros((rows // 4, LANES), F32)
        for part in range(2):
            pick = jnp.logical_and(lane // wide == part, row - rank == lane - part * wide)
            start = (2 * g + part) * (rows // 4)
            total = total + dot_nn(low_ref[start:start + rows // 4, :], one_hot(pick))
        low_pack[g] = total.astype(BF16)
        low_copy(g).start()

    def modulate(i, carry):
        span = pl.ds(pl.multiple_of(i * block, block), block)
        pltpu.make_async_copy(hidden_hbm.at[0, span], x_ref.at[span], load.at[i]).wait()
        x = x_ref[span, :].astype(F32)
        mean = jnp.sum(x, axis=1, keepdims=True) * (1.0 / width)
        centred = x - mean
        variance = jnp.sum(centred * centred, axis=1, keepdims=True) * (1.0 / width)
        normed = centred * lax.rsqrt(variance + 1e-06)
        x_low = (normed * (1.0 + mod_ref[1:2, :]) + mod_ref[0:1, :]).astype(BF16)
        x_ref[span, :] = x_low
        low_ref[span, :] = dot_nt(x_low, down_ref[...]).astype(BF16)
        return carry

    half_blocks = blocks // 2
    lax.fori_loop(0, half_blocks, modulate, 0)
    pack_low(0)
    lax.fori_loop(half_blocks, blocks - 1, modulate, 0)
    pump(0)
    lax.fori_loop(blocks - 1, blocks, modulate, 0)
    pack_low(1)
    for c in range(EARLY, 2 * PARTS):
        swap(c // PARTS, c % PARTS).start()

    def send_rest(h, carry):
        for part in range(PARTS):
            swap(h, part).start()
        return carry

    lax.fori_loop(2, heads, send_rest, 0)
    for copy in others[2:]:
        copy.start()
    pump(1)
    for copy in others[2:]:
        copy.wait()

    def build(h, carry):
        lanes = pl.ds(pl.multiple_of(h * HEAD, HEAD), HEAD)
        for j in range(3):
            ups[h, j * rank:(j + 1) * rank, j * HEAD:(j + 1) * HEAD] = (
                up_ref[j * rank:(j + 1) * rank, lanes])
        return carry

    lax.fori_loop(0, heads, build, 0)
    pump(2)
    pump(3)
    for g in range(2):
        low_copy(g).wait_recv()

        @pl.when(relay_out)
        def _(g=g):
            low_next(g).start()

    inside = jnp.logical_and(lane >= rank, lane < 3 * rank)

    def unpack_low(s, dst):
        quarter = rows // 4
        for part in range(2):
            pick = jnp.logical_and(inside, row == lane - rank + part * wide)
            select = one_hot(pick)
            for g in range(2):
                start = (2 * g + part) * quarter
                dst[start:start + quarter, :] = dot_nn(low_got[2 * s + g], select).astype(BF16)

    unpack_low(0, low_swap)
    for c in range(PARTS, AHEAD):
        pump(c)

    @pl.when(relay_in)
    def _():
        for g in range(2):
            low_next(g).wait_recv()
        unpack_low(1, low_relay)

    def value_return(s):
        return remote(r_out.at[s], r_in.at[s], r_send.at[s], r_recv.at[s], (partner, other)[s])

    def key_return(s):
        return remote(r_out.at[2 + s], r_in.at[2 + s], r_send.at[2 + s], r_recv.at[2 + s],
                      (partner, other)[s])

    def send_back(ready, start):
        base = 0 if ready is value_return else 2
        for s in range(2):
            r_out[base + s] = rkv[start:start + rank, (s + 1) * rows:(s + 2) * rows].astype(BF16)
        ready(0).start()

        @pl.when(relay_in)
        def _():
            ready(1).start()

    def take_back(ready, start):
        base = 0 if ready is value_return else 2
        ready(0).wait_recv()

        @pl.when(relay_in)
        def _():
            ready(1).wait_recv()

        return (rkv[start:start + rank, 0:rows] + r_in[base].astype(F32)
                + r_in[base + 1].astype(F32)).astype(BF16)

    for s, low in enumerate((low_ref, low_swap, low_relay)):
        kl[s * rows:(s + 1) * rows, HEAD:] = low[...]
        vl[s * rows:(s + 1) * rows, HEAD:] = low[...]


    def att_copy(h):
        lanes = pl.ds(pl.multiple_of(h * HEAD, HEAD), HEAD)
        return pltpu.make_async_copy(att_ref.at[h], att_hbm.at[0, :, lanes], att_sem.at[h])

    def pump_next(h, part):
        c = h * PARTS + AHEAD + part

        @pl.when(c < chunks)
        def _():
            pump(c)

    def arrive(h, part):
        @pl.when(relay_in)
        def _():
            for i in range(2):
                relay(h * PARTS + 2 * part + i).wait_recv()

    def one_head(h, carry):
        lanes = pl.ds(pl.multiple_of(h * HEAD, HEAD), HEAD)
        own = dot_nn(low_ref[...], ups[h])
        q_ref[...] = (fq_ref[0, :, lanes].astype(F32) + own[:, 0:HEAD]).astype(BF16)
        kl[0:rows, 0:HEAD] = (fk_ref[0, :, lanes].astype(F32) + own[:, HEAD:2 * HEAD]).astype(BF16)
        vl[0:rows, 0:HEAD] = (fv_ref[0, :, lanes].astype(F32) + own[:, 2 * HEAD:]).astype(BF16)

        arrive(h, 0)
        arrive(h, 1)
        for s, (low, got) in enumerate(((low_swap, swap_ref), (low_relay, relay_ref))):
            add = dot_nn(low[...], ups[h, :, HEAD:])
            span = slice((s + 1) * rows, (s + 2) * rows)
            kl[span, 0:HEAD] = (got[h, 0].astype(F32) + add[:, 0:HEAD]).astype(BF16)
            vl[span, 0:HEAD] = (got[h, 1].astype(F32) + add[:, HEAD:]).astype(BF16)
        for t in range(rows // TILE):
            span = slice(t * TILE, (t + 1) * TILE)
            scores = dot_nt(q_ref[span, :], kl[:, 0:HEAD]) * scale_two + bias_ref[t:t + 1, :]
            top = jnp.max(scores, axis=1, keepdims=True)
            weights = jnp.exp2(scores - top)
            inverse = 1.0 / jnp.sum(weights, axis=1, keepdims=True)
            probs = weights * inverse
            prob_grad = dot_nt(g_ref[0, span, lanes], vl[:, 0:HEAD])
            centre = jnp.sum(probs * prob_grad, axis=1, keepdims=True)
            probs_s[span, :] = probs.astype(BF16)
            grad_s[span, :] = (probs * (prob_grad - centre) * scale_root).astype(BF16)
            if t == 1:
                pump_next(h, 0)
        pump_next(h, 1)
        q_all = q_ref[...]
        g_all = g_ref[0, :, lanes]
        q_up = dot_nt(up_ref[rank:2 * rank, lanes], q_all).astype(BF16)
        g_up = dot_nt(up_ref[2 * rank:3 * rank, lanes], g_all).astype(BF16)
        rkv[0:rank, :] += dot_nn(q_up, grad_s[...])
        rkv[rank:2 * rank, :] += dot_nn(g_up, probs_s[...])
        att = dot_nn(probs_s[...], vl[...])
        att_ref[h] = att[:, 0:HEAD].astype(BF16)
        att_copy(h).start()
        low_v = att[:, HEAD:].astype(BF16)
        dq = dot_nn(grad_s[...], kl[...])
        dq_low = dq[:, 0:HEAD].astype(BF16)
        low_k = dq[:, HEAD:].astype(BF16)
        rq_ref[...] += dot_nt(up_ref[0:rank, lanes], dq_low)
        ups_terms = (dot_tn(low_ref[...], dq_low), dot_tn(low_k, q_all), dot_tn(low_v, g_all))
        for j, term in enumerate(ups_terms):
            for r in range(rank // ROWS):
                start = j * rank + r * ROWS
                spot = h * (3 * rank // ROWS) + start // ROWS
                up_terms[spot] = (term[start:start + ROWS] * norm_factor).astype(BF16)
        pump_next(h, 2)
        pump_next(h, 3)
        return carry

    lax.fori_loop(0, heads, one_head, 0)
    send_back(value_return, rank)
    send_back(key_return, 0)

    def down_dot(total, grads, count):
        def columns(i, carry):
            lanes = pl.ds(pl.multiple_of(i * 2 * LANES, 2 * LANES), 2 * LANES)
            term = dot_nn(grads, x_ref[:, lanes]) * norm_factor
            for l in range(2):
                for r in range(count):
                    total.terms[(i * 2 + l) * count + r] = (
                        term[r * ROWS:(r + 1) * ROWS, l * LANES:(l + 1) * LANES].astype(BF16))
            return carry

        lax.fori_loop(0, width // (2 * LANES), columns, 0)

    one = (rank // ROWS) * (width // LANES)
    kept = first_tiles - 2 * one
    if kept:
        first.terms[2 * one:first_tiles] = up_terms[0:kept]
    if later_tiles > one:
        later.terms[one:later_tiles] = up_terms[kept:]
    grads = jnp.concatenate([rq_ref[...].astype(BF16), take_back(value_return, rank)], axis=0)
    down_dot(first, grads, 2 * rank // ROWS)
    first.pair_start()
    grads = take_back(key_return, 0)
    down_dot(later, grads, rank // ROWS)
    later.pair_start()
    first.xy_start()
    later.xy_start()
    first.z_start()
    later.z_start()
    first.z_back()
    later.z_back()
    first.xy_back()
    later.xy_back()
    first.pair_back()
    later.pair_back()
    first.finish()
    later.finish()

    for g in range(2):
        low_copy(g).wait_send()

    @pl.when(relay_out)
    def _():
        for g in range(2):
            low_next(g).wait_send()

    def swap_sent(h, carry):
        for part in range(PARTS):
            swap(h, part).wait_send()
        return carry

    lax.fori_loop(0, heads, swap_sent, 0)

    @pl.when(relay_out)
    def _():
        lax.fori_loop(0, chunks, lambda c, carry: (relay(c).wait_send(), carry)[1], 0)

    for ready in (value_return, key_return):
        ready(0).wait_send()

    @pl.when(relay_in)
    def _():
        for ready in (value_return, key_return):
            ready(1).wait_send()

    lax.fori_loop(0, heads, lambda h, carry: (att_copy(h).wait(), carry)[1], 0)
    first.drain()
    later.drain()


def fused(nb, nt, norm_factor, step, window, hidden, modulation, down, up, fq, fk, fv, g):
    _, rows, width = hidden.shape
    across = fq.shape[2]
    heads = across // HEAD
    rank = up.shape[0] // 3
    dma = pltpu.SemaphoreType.DMA
    vmem = pltpu.VMEM
    smem = pl.BlockSpec(memory_space=pltpu.SMEM)
    anywhere = pl.BlockSpec(memory_space=pl.ANY)
    whole = pl.BlockSpec(memory_space=pltpu.VMEM)
    chunks = PARTS * heads
    blocks = rows // TILE
    first_tiles, later_tiles = split_tiles(rank, width, heads, nb, nt)
    totals = [share_of(tiles, nb, nt) * nb * nt for tiles in (first_tiles, later_tiles)]
    return pl.pallas_call(
        functools.partial(fused_kernel, nb, nt, rank, norm_factor),
        out_shape=[
            jax.ShapeDtypeStruct((1, rows, across), BF16),
            jax.ShapeDtypeStruct((totals[0], ROWS, LANES), BF16),
            jax.ShapeDtypeStruct((totals[1], ROWS, LANES), BF16),
        ],
        in_specs=[smem, smem] + [anywhere] * 8,
        out_specs=[anywhere, whole, whole],
        scratch_shapes=[
            vmem((rows, width), BF16), vmem(modulation.shape, F32), vmem((2, width), F32),
            vmem((LANES, width), BF16), vmem(up.shape, BF16), vmem((heads, LANES, 3 * HEAD), BF16),
            vmem(fq.shape, BF16), vmem(fq.shape, BF16), vmem(fq.shape, BF16), vmem(fq.shape, BF16),
            vmem((heads, 2, rows, HEAD), BF16), vmem((heads, 2, rows, HEAD), BF16),
            vmem((2, rows // 4, LANES), BF16), vmem((4, rows // 4, LANES), BF16),
            vmem((rows, LANES), BF16), vmem((rows, LANES), BF16), vmem((rows, LANES), BF16),
            vmem((8, 3 * rows), F32), vmem((rows, HEAD), BF16),
            vmem((3 * rows, 2 * HEAD), BF16), vmem((3 * rows, 2 * HEAD), BF16),
            vmem((rows, 3 * rows), BF16), vmem((rows, 3 * rows), BF16),
            vmem((2 * rank, 3 * rows), F32), vmem((rank, rows), F32),
            vmem((4, rank, rows), BF16), vmem((4, rank, rows), BF16),
            vmem((heads, rows, HEAD), BF16), vmem((heads * (3 * rank // ROWS), ROWS, LANES), BF16),
            dma((blocks + 7,)), dma((heads,)),
            dma((chunks,)), dma((chunks,)), dma((chunks,)), dma((chunks,)),
            dma((4,)), dma((4,)), dma((4,)), dma((4,)),
        ] + sum_shapes(first_tiles, nb, nt) + sum_shapes(later_tiles, nb, nt),
        compiler_params=pltpu.CompilerParams(
            collective_id=0, has_side_effects=True, vmem_limit_bytes=60 << 20
        ),
        name="fused",
    )(step, window, hidden, modulation, down, up, fq, fk, fv, g)


def place_kernel(rank, att_hbm, first_hbm, later_hbm, att_out, down_out, up_out,
                 att_ref, first_ref, later_ref, down_ref, up_ref, load, store):
    rows, across = att_ref.shape[1:]
    heads = across // HEAD
    width = down_ref.shape[1]
    one = (rank // ROWS) * (width // LANES)
    parts = 4
    cut = rows // parts
    takes = [pltpu.make_async_copy(first_hbm, first_ref, load.at[0]),
             pltpu.make_async_copy(later_hbm, later_ref, load.at[1])]
    moves = [(pltpu.make_async_copy(att_hbm.at[:, pl.ds(i * cut, cut)],
                                    att_ref.at[:, pl.ds(i * cut, cut)], load.at[2 + i]),
              pltpu.make_async_copy(att_ref.at[:, pl.ds(i * cut, cut)],
                                    att_out.at[:, pl.ds(i * cut, cut)], store.at[2 + i]))
             for i in range(parts)]
    for copy in takes:
        copy.start()
    for copy, _ in moves:
        copy.start()
    for copy in takes:
        copy.wait()
    step = rank // ROWS
    for l in range(width // LANES):
        lanes = slice(l * LANES, (l + 1) * LANES)
        for r in range(step):
            spots = (first_ref[l * 2 * step + r], later_ref[l * step + r],
                     first_ref[l * 2 * step + step + r])
            for j, tile in enumerate(spots):
                down_ref[j * rank + r * ROWS:j * rank + (r + 1) * ROWS, lanes] = tile.astype(F32)
    down_store = pltpu.make_async_copy(down_ref, down_out, store.at[0])
    down_store.start()
    spare = min(3 * step * heads, later_ref.shape[0] - one)
    kept = 3 * step * heads - spare
    for h in range(heads):
        lanes = slice(h * HEAD, (h + 1) * HEAD)
        for r in range(3 * step):
            k = h * 3 * step + r
            tile = first_ref[2 * one + k] if k < kept else later_ref[one + k - kept]
            up_ref[r * ROWS:(r + 1) * ROWS, lanes] = tile.astype(F32)
    up_store = pltpu.make_async_copy(up_ref, up_out, store.at[1])
    up_store.start()
    for copy, then in moves:
        copy.wait()
        then.start()
    for _, then in moves:
        then.wait()
    down_store.wait()
    up_store.wait()


def put_in_place(rank, width, attended, first, later):
    across = attended.shape[2]
    vmem, dma = pltpu.VMEM, pltpu.SemaphoreType.DMA
    anywhere = pl.BlockSpec(memory_space=pl.ANY)
    return pl.pallas_call(
        functools.partial(place_kernel, rank),
        out_shape=[
            jax.ShapeDtypeStruct(attended.shape, BF16),
            jax.ShapeDtypeStruct((3 * rank, width), F32),
            jax.ShapeDtypeStruct((3 * rank, across), F32),
        ],
        in_specs=[anywhere] * 3,
        out_specs=[anywhere] * 3,
        scratch_shapes=[
            vmem(attended.shape, BF16), vmem(first.shape, BF16), vmem(later.shape, BF16),
            vmem((3 * rank, width), F32), vmem((3 * rank, across), F32), dma((6,)), dma((6,)),
        ],
        name="place",
    )(attended, first, later)


def per_device(
    hidden,
    frozen_queries,
    frozen_keys,
    frozen_values,
    reward_output_gradient,
    truncation_step,
    modulation,
    adapter_down_weight,
    adapter_up_weight,
    window,
):
    slab_rows, width = hidden.shape[1:]
    across = frozen_queries.shape[2]
    rank = adapter_up_weight.shape[1]
    nb, nt = lax.axis_size("batch"), lax.axis_size("tiles")
    norm_factor = 1.0 / math.sqrt(hidden.shape[0] * nb * slab_rows * nt)
    down = adapter_down_weight.transpose(0, 2, 1).reshape(3 * rank, width)
    up = adapter_up_weight.reshape(3 * rank, across)
    attended, first, later = fused(
        nb, nt, norm_factor, truncation_step, window, hidden, modulation, down, up,
        frozen_queries, frozen_keys, frozen_values, reward_output_gradient,
    )
    attended, grad_down, grad_up = put_in_place(rank, width, attended, first, later)
    grad_down = grad_down.reshape(3, rank, width).transpose(0, 2, 1)
    grad_up = grad_up.reshape(3, rank, across)
    return (attended, grad_down, grad_up)


def solution(mesh):
    placed = (
        P("batch", "tiles", None),
        P("batch", "tiles", None),
        P("batch", "tiles", None),
        P("batch", "tiles", None),
        P("batch", "tiles", None),
        P("batch"),
        P(),
        P(),
        P(),
        P("tiles", None),
    )
    return jax.shard_map(
        per_device,
        mesh=mesh,
        in_specs=placed,
        out_specs=(P("batch", "tiles", None), P(), P()),
        check_vma=False,
    )
```

```python
import functools
import math

import jax
import jax.numpy as jnp
from jax import lax
from jax.experimental import pallas as pl
from jax.experimental.pallas import tpu as pltpu
from jax.sharding import PartitionSpec as P

HEAD = 128
TILE = 128
GF = 2
GR = 2
LANES = 128
ROWS = 16
PARTS = 4
EARLY = 4
AHEAD = 7
BF16 = jnp.bfloat16
F32 = jnp.float32


def dot_nt(a, b):
    return lax.dot_general(
        a, b, (((1,), (1,)), ((), ())), preferred_element_type=jnp.float32
    )


def dot_tn(a, b):
    return lax.dot_general(
        a, b, (((0,), (0,)), ((), ())), preferred_element_type=jnp.float32
    )


def dot_nn(a, b):
    return jnp.dot(a, b, preferred_element_type=jnp.float32)


def remote(src, dst, send, recv, peer):
    return pltpu.make_async_remote_copy(
        src_ref=src, dst_ref=dst, send_sem=send, recv_sem=recv,
        device_id=peer, device_id_type=pl.DeviceIdType.MESH,
    )


class Place:
    def __init__(self, nb, nt):
        self.nb, self.nt = nb, nt
        self.nx, self.nz = nb // 2, nt // 2
        self.nxy = 2 * self.nx
        b, t = lax.axis_index("batch"), lax.axis_index("tiles")
        self.b, self.t = b, t
        self.core, self.x = lax.rem(b, 2), b // 2
        self.y, self.z = lax.rem(t, 2), t // 2

    def core_peer(self):
        return {"batch": self.b + 1 - 2 * self.core}

    def xy_offset(self, d, sign):
        dx, dy = d // 2, d % 2
        x = lax.rem(self.x + sign * dx + self.nx, self.nx)
        return x, lax.rem(self.y + dy, 2)

    def xy_peer(self, d):
        x, y = self.xy_offset(d, 1)
        return {"batch": x * 2 + self.core, "tiles": self.z * 2 + y}

    def xy_index(self, d, sign):
        x, y = self.xy_offset(d, sign)
        return x * 2 + y

    def z_peer(self, e):
        return {"tiles": lax.rem(self.z + e, self.nz) * 2 + self.y}


def share_of(tiles, nb, nt):
    return -(-tiles // (nb * nt))


def split_tiles(rank, width, heads, nb, nt):
    one = (rank // ROWS) * (width // LANES)
    ups = (3 * rank // ROWS) * heads
    early = (ups - 3 * rank // ROWS) // (nb * nt) * (nb * nt)
    return early, 2 * one, one + ups - early


def sum_shapes(tiles, nb, nt):
    share = share_of(tiles, nb, nt)
    nxy, nz = nb, nt // 2
    quarter = nz * share
    total = nb * nt * share
    dma = pltpu.SemaphoreType.DMA
    return [
        pltpu.VMEM((total, ROWS, LANES), BF16),
        pltpu.VMEM((total // 2, ROWS, LANES), BF16),
        pltpu.VMEM((nxy - 1, quarter, ROWS, LANES), BF16),
        pltpu.VMEM((nxy - 1, quarter, ROWS, LANES), BF16),
        pltpu.VMEM((quarter, ROWS, LANES), F32),
        pltpu.VMEM((nz - 1, share, ROWS, LANES), BF16),
        pltpu.VMEM((nz - 1, share, ROWS, LANES), BF16),
        dma((nxy,)), dma((nxy,)), dma((nxy - 1,)), dma((nxy - 1,)),
        dma((nz - 1,)), dma((nz - 1,)), dma((nz - 1,)), dma((nz - 1,)),
        dma((nxy - 1, nz)), dma((nxy - 1, nz)), dma((nxy, nz)), dma((nxy, nz)),
    ]


class Sum:
    def __init__(self, place, tiles, out, refs):
        self.place, self.tiles, self.out = place, tiles, out
        (self.terms, self.pair, self.part1, self.got1, self.acc, self.part2, self.got2,
         self.s0, self.r0, self.s1, self.r1, self.s2, self.r2, self.s3, self.r3,
         self.s4, self.r4, self.s5, self.r5) = refs
        self.share = share_of(tiles, place.nb, place.nt)
        self.quarter = place.nz * self.share
        self.half = place.nxy * self.quarter
        self.mine = place.core * self.half
        self.order = list(range(place.nxy - 1, -1, -1))
        self.sent = []

    def clear(self):
        pad = self.terms.shape[0] - self.tiles
        if pad:
            self.terms[self.tiles:] = jnp.zeros((pad, ROWS, LANES), BF16)

    def go(self, *args):
        copy = remote(*args)
        copy.start()
        self.sent.append(copy)
        return copy

    def pair_start(self):
        p = self.place
        other = (1 - p.core) * self.half
        self.c0 = {}
        for d in self.order:
            q = p.xy_index(d, 1) * self.quarter
            self.c0[d] = self.go(self.terms.at[pl.ds(other + q, self.quarter)],
                                 self.pair.at[pl.ds(q, self.quarter)],
                                 self.s0.at[d], self.r0.at[d], p.core_peer())

    def xy_start(self):
        p = self.place
        self.c1 = {}
        for d in self.order:
            q = p.xy_index(d, 1) * self.quarter
            self.c0[d].wait_recv()
            total = (self.terms[pl.ds(self.mine + q, self.quarter)].astype(F32)
                     + self.pair[pl.ds(q, self.quarter)].astype(F32))
            if d == 0:
                self.acc[...] = total
            else:
                self.part1[d - 1] = total.astype(BF16)
                self.c1[d] = self.go(self.part1.at[d - 1], self.got1.at[d - 1],
                                     self.s1.at[d - 1], self.r1.at[d - 1], p.xy_peer(d))

    def z_start(self):
        p = self.place
        for d in self.order:
            if d:
                self.c1[d].wait_recv()
        total = self.acc[...]
        for d in range(1, p.nxy):
            total = total + self.got1[d - 1].astype(F32)
        self.acc[...] = total
        self.c2 = []
        for e in range(1, p.nz):
            spot = lax.rem(p.z + e, p.nz) * self.share
            self.part2[e - 1] = self.acc[pl.ds(spot, self.share)].astype(BF16)
            self.c2.append(self.go(self.part2.at[e - 1], self.got2.at[e - 1],
                                   self.s2.at[e - 1], self.r2.at[e - 1], p.z_peer(e)))

    def spot(self, d, e):
        p = self.place
        plane = lax.rem(p.z - e + p.nz, p.nz) * self.share
        return self.out.at[pl.ds(self.mine + p.xy_index(d, -1) * self.quarter + plane, self.share)]

    def z_back(self):
        p = self.place
        total = self.acc[pl.ds(p.z * self.share, self.share)]
        for e in range(1, p.nz):
            self.c2[e - 1].wait_recv()
            total = total + self.got2[e - 1].astype(F32)
        mine = self.spot(0, 0)
        mine[...] = total.astype(BF16)
        self.c3 = [self.go(mine, mine, self.s3.at[e - 1], self.r3.at[e - 1], p.z_peer(e))
                   for e in range(1, p.nz)]

    def xy_back(self):
        p = self.place
        self.c4, self.c5 = {}, []
        for e in range(p.nz):
            if e:
                self.c3[e - 1].wait_recv()
            piece = self.spot(0, e)
            for d in self.order:
                if d:
                    self.c4[d, e] = self.go(piece, piece, self.s4.at[d - 1, e],
                                            self.r4.at[d - 1, e], p.xy_peer(d))
            self.c5.append(self.go(piece, piece, self.s5.at[0, e], self.r5.at[0, e],
                                   p.core_peer()))

    def pair_back(self):
        p = self.place
        for e in range(p.nz):
            for d in range(1, p.nxy):
                self.c4[d, e].wait_recv()
                piece = self.spot(d, e)
                self.c5.append(self.go(piece, piece, self.s5.at[d, e], self.r5.at[d, e],
                                       p.core_peer()))

    def finish(self):
        for copy in self.c5:
            copy.wait_recv()

    def drain(self):
        for copy in self.sent:
            copy.wait_send()


def fused_kernel(nb, nt, rank, norm_factor, step_ref, window_ref, hidden_hbm, mod_hbm, down_hbm, up_hbm,
                 fq_hbm, fk_hbm, fv_hbm, g_hbm,
                 att_hbm, early_out, first_out, later_out,
                 x_ref, mod_all, mod_ref, down_ref, up_ref, ups, fq_ref, fk_ref, fv_ref, g_ref,
                 swap_ref, relay_ref, low_pack, low_got, low_ref, low_swap, low_relay, bias_ref, q_ref, kl, vl,
                 probs_f, probs_s, grad_s, rkv, rq_ref, r_out, r_in, att_ref, up_terms,
                 load, att_sem, swap_send, swap_recv, relay_send, relay_recv,
                 low_send, low_recv, r_send, r_recv, *sums):
    place = Place(nb, nt)
    t_index, odd = place.t, place.y
    rows, across = fq_ref.shape[1:]
    heads = across // HEAD
    width = x_ref.shape[1]
    half = rows // 2
    chunks = PARTS * heads
    per = len(sums) // 3
    counts = split_tiles(rank, width, heads, nb, nt)
    outs = (early_out, first_out, later_out)
    early, first, later = [Sum(place, counts[i], outs[i], sums[i * per:(i + 1) * per])
                           for i in range(3)]
    early_tiles = counts[0]

    partner = {"tiles": t_index + 1 - 2 * odd}
    target = {"tiles": lax.rem(t_index + 2 - 4 * odd + nt, nt)}
    other = {"tiles": lax.rem(t_index - 1 + 2 * odd + nt, nt)}
    even = odd == 0
    relay_in = jnp.where(even, t_index >= 2, t_index < nt - 2)
    relay_out = jnp.where(even, t_index < nt - 2, t_index >= 2)

    blocks = rows // TILE
    block = TILE
    hidden_loads = [
        pltpu.make_async_copy(hidden_hbm.at[0, pl.ds(i * block, block)],
                              x_ref.at[pl.ds(i * block, block)], load.at[i])
        for i in range(blocks)
    ]
    others = [
        pltpu.make_async_copy(src, dst, load.at[blocks + i])
        for i, (src, dst) in enumerate((
            (mod_hbm, mod_all), (down_hbm, down_ref.at[pl.ds(0, 3 * rank)]),
            (up_hbm, up_ref),
            (fq_hbm, fq_ref), (fk_hbm, fk_ref), (fv_hbm, fv_ref), (g_hbm, g_ref)))
    ]

    barrier = pltpu.get_barrier_semaphore()
    greet = [place.core_peer(), other]
    greet += [place.xy_peer(d) for d in range(1, place.nxy)]
    greet += [place.z_peer(e) for e in range(1, place.nz)]
    for peer in greet:
        pl.semaphore_signal(barrier, inc=1, device_id=peer, device_id_type=pl.DeviceIdType.MESH)
    hidden_loads[0].start()
    for copy in others[:2]:
        copy.start()
    for copy in hidden_loads[1:]:
        copy.start()

    scale_root = 1.0 / math.sqrt(HEAD)
    scale_two = scale_root * math.log2(math.e)
    per_slab = GF * GR
    sides = (jnp.int32(9), 18 * (1 - odd), 18 * odd)
    for s, side in enumerate(sides):
        for t in range(per_slab):
            for u in range(per_slab):
                code = side + 3 * (u // GR - t // GR + 1) + u % GR - t % GR + 1
                value = jnp.where(window_ref[t, code] > 0, 0.0, -1e30).astype(F32)
                if s == 2:
                    value = jnp.where(relay_in, value, -1e30)
                spot = (s * per_slab + u) * TILE
                bias_ref[t:t + 1, spot:spot + TILE] = jnp.full((1, TILE), value, F32)

    pl.semaphore_wait(barrier, len(greet))

    def swap(h, part):
        src = (fk_hbm, fv_hbm)[part // 2]
        start = (part % 2) * half
        lanes = pl.ds(pl.multiple_of(h * HEAD, HEAD), HEAD)
        c = h * PARTS + part
        return remote(src.at[0, pl.ds(start, half), lanes],
                      swap_ref.at[h, part // 2, pl.ds(start, half)],
                      swap_send.at[c], swap_recv.at[c], partner)

    def chunk(ref, c):
        return ref.at[c // PARTS, lax.rem(c, PARTS) // 2, pl.ds(lax.rem(c, 2) * half, half)]

    def relay(c):
        return remote(chunk(swap_ref, c), chunk(relay_ref, c), relay_send.at[c], relay_recv.at[c],
                      target)

    def pump(c):
        remote(chunk(swap_ref, c), chunk(swap_ref, c), swap_send.at[c], swap_recv.at[c],
               partner).wait_recv()

        @pl.when(relay_out)
        def _():
            relay(c).start()

    for c in range(EARLY):
        swap(c // PARTS, c % PARTS).start()

    @pl.when(jnp.logical_not(relay_in))
    def _():
        low_relay[...] = jnp.zeros_like(low_relay)

        def clear(h, carry):
            relay_ref[h] = jnp.zeros(relay_ref.shape[1:], BF16)
            return carry

        lax.fori_loop(0, heads, clear, 0)
        for j in range(2):
            r_in[2 * j + 1] = jnp.zeros(r_in.shape[1:], BF16)

    early.clear()
    first.clear()
    later.clear()
    rq_ref[...] = jnp.zeros_like(rq_ref)
    rkv[...] = jnp.zeros_like(rkv)
    ups[...] = jnp.zeros_like(ups)
    down_ref[3 * rank:LANES] = jnp.zeros((LANES - 3 * rank, width), BF16)

    for copy in others[:2]:
        copy.wait()
    mod_ref[...] = mod_all[step_ref[0]]
    row = lax.broadcasted_iota(jnp.int32, (LANES, LANES), 0)
    lane = lax.broadcasted_iota(jnp.int32, (LANES, LANES), 1)
    wide = 2 * rank

    def low_copy(g):
        return remote(low_pack.at[g], low_got.at[g], low_send.at[g], low_recv.at[g], partner)

    def low_next(g):
        return remote(low_got.at[g], low_got.at[2 + g], low_send.at[2 + g], low_recv.at[2 + g],
                      target)

    def one_hot(pick):
        return jnp.where(pick, 1.0, 0.0).astype(BF16)

    def pack_low(g):
        total = jnp.zeros((rows // 4, LANES), F32)
        for part in range(2):
            pick = jnp.logical_and(lane // wide == part, row - rank == lane - part * wide)
            start = (2 * g + part) * (rows // 4)
            total = total + dot_nn(low_ref[start:start + rows // 4, :], one_hot(pick))
        low_pack[g] = total.astype(BF16)
        low_copy(g).start()

    def modulate(i, carry):
        span = pl.ds(pl.multiple_of(i * block, block), block)
        pltpu.make_async_copy(hidden_hbm.at[0, span], x_ref.at[span], load.at[i]).wait()
        x = x_ref[span, :].astype(F32)
        mean = jnp.sum(x, axis=1, keepdims=True) * (1.0 / width)
        centred = x - mean
        variance = jnp.sum(centred * centred, axis=1, keepdims=True) * (1.0 / width)
        normed = centred * lax.rsqrt(variance + 1e-06)
        x_low = (normed * (1.0 + mod_ref[1:2, :]) + mod_ref[0:1, :]).astype(BF16)
        x_ref[span, :] = x_low
        low_ref[span, :] = dot_nt(x_low, down_ref[...]).astype(BF16)
        return carry

    half_blocks = blocks // 2
    lax.fori_loop(0, half_blocks, modulate, 0)
    pack_low(0)
    lax.fori_loop(half_blocks, blocks - 1, modulate, 0)
    pump(0)
    lax.fori_loop(blocks - 1, blocks, modulate, 0)
    pack_low(1)
    for c in range(EARLY, 2 * PARTS):
        swap(c // PARTS, c % PARTS).start()

    def send_rest(h, carry):
        for part in range(PARTS):
            swap(h, part).start()
        return carry

    lax.fori_loop(2, heads, send_rest, 0)
    for copy in others[2:]:
        copy.start()
    pump(1)
    for copy in others[2:]:
        copy.wait()

    def build(h, carry):
        lanes = pl.ds(pl.multiple_of(h * HEAD, HEAD), HEAD)
        for j in range(3):
            ups[h, j * rank:(j + 1) * rank, j * HEAD:(j + 1) * HEAD] = (
                up_ref[j * rank:(j + 1) * rank, lanes])
        return carry

    lax.fori_loop(0, heads, build, 0)
    pump(2)
    pump(3)
    for g in range(2):
        low_copy(g).wait_recv()

        @pl.when(relay_out)
        def _(g=g):
            low_next(g).start()

    inside = jnp.logical_and(lane >= rank, lane < 3 * rank)

    def unpack_low(s, dst):
        quarter = rows // 4
        for part in range(2):
            pick = jnp.logical_and(inside, row == lane - rank + part * wide)
            select = one_hot(pick)
            for g in range(2):
                start = (2 * g + part) * quarter
                dst[start:start + quarter, :] = dot_nn(low_got[2 * s + g], select).astype(BF16)

    unpack_low(0, low_swap)
    for c in range(PARTS, AHEAD):
        pump(c)

    @pl.when(relay_in)
    def _():
        for g in range(2):
            low_next(g).wait_recv()
        unpack_low(1, low_relay)

    def value_return(s):
        return remote(r_out.at[s], r_in.at[s], r_send.at[s], r_recv.at[s], (partner, other)[s])

    def key_return(s):
        return remote(r_out.at[2 + s], r_in.at[2 + s], r_send.at[2 + s], r_recv.at[2 + s],
                      (partner, other)[s])

    def send_back(ready, start):
        base = 0 if ready is value_return else 2
        for s in range(2):
            r_out[base + s] = rkv[start:start + rank, (s + 1) * rows:(s + 2) * rows].astype(BF16)
        ready(0).start()

        @pl.when(relay_in)
        def _():
            ready(1).start()

    def take_back(ready, start):
        base = 0 if ready is value_return else 2
        ready(0).wait_recv()

        @pl.when(relay_in)
        def _():
            ready(1).wait_recv()

        return (rkv[start:start + rank, 0:rows] + r_in[base].astype(F32)
                + r_in[base + 1].astype(F32)).astype(BF16)

    for s, low in enumerate((low_ref, low_swap, low_relay)):
        kl[s * rows:(s + 1) * rows, HEAD:] = low[...]
        vl[s * rows:(s + 1) * rows, HEAD:] = low[...]


    def att_copy(h):
        lanes = pl.ds(pl.multiple_of(h * HEAD, HEAD), HEAD)
        return pltpu.make_async_copy(att_ref.at[h], att_hbm.at[0, :, lanes], att_sem.at[h])

    def pump_next(h, part):
        c = h * PARTS + AHEAD + part

        @pl.when(c < chunks - 2)
        def _():
            pump(c)

    def arrive(h, part):
        @pl.when(relay_in)
        def _():
            for i in range(2):
                relay(h * PARTS + 2 * part + i).wait_recv()

    def own_rows(h, lanes):
        own = dot_nn(low_ref[...], ups[h])
        q_ref[...] = (fq_ref[0, :, lanes].astype(F32) + own[:, 0:HEAD]).astype(BF16)
        kl[0:rows, 0:HEAD] = (fk_ref[0, :, lanes].astype(F32) + own[:, HEAD:2 * HEAD]).astype(BF16)
        vl[0:rows, 0:HEAD] = (fv_ref[0, :, lanes].astype(F32) + own[:, 2 * HEAD:]).astype(BF16)

    def softmax(t):
        span = slice(t * TILE, (t + 1) * TILE)
        scores = dot_nt(q_ref[span, :], kl[:, 0:HEAD]) * scale_two + bias_ref[t:t + 1, :]
        top = jnp.max(scores, axis=1, keepdims=True)
        weights = jnp.exp2(scores - top)
        inverse = 1.0 / jnp.sum(weights, axis=1, keepdims=True)
        probs = weights * inverse
        probs_s[span, :] = probs.astype(BF16)
        return probs

    def score_grads(t, lanes, probs):
        span = slice(t * TILE, (t + 1) * TILE)
        prob_grad = dot_nt(g_ref[0, span, lanes], vl[:, 0:HEAD])
        centre = jnp.sum(probs * prob_grad, axis=1, keepdims=True)
        grad_s[span, :] = (probs * (prob_grad - centre) * scale_root).astype(BF16)

    def key_sums(lanes):
        q_up = dot_nt(up_ref[rank:2 * rank, lanes], q_ref[...]).astype(BF16)
        rkv[0:rank, :] += dot_nn(q_up, grad_s[...])

    def value_sums(lanes):
        g_up = dot_nt(up_ref[2 * rank:3 * rank, lanes], g_ref[0, :, lanes]).astype(BF16)
        rkv[rank:2 * rank, :] += dot_nn(g_up, probs_s[...])

    def outputs(h, lanes):
        q_all = q_ref[...]
        g_all = g_ref[0, :, lanes]
        att = dot_nn(probs_s[...], vl[...])
        att_ref[h] = att[:, 0:HEAD].astype(BF16)
        att_copy(h).start()
        low_v = att[:, HEAD:].astype(BF16)
        dq = dot_nn(grad_s[...], kl[...])
        dq_low = dq[:, 0:HEAD].astype(BF16)
        low_k = dq[:, HEAD:].astype(BF16)
        rq_ref[...] += dot_nt(up_ref[0:rank, lanes], dq_low)
        ups_terms = (dot_tn(low_ref[...], dq_low), dot_tn(low_k, q_all), dot_tn(low_v, g_all))
        for j, term in enumerate(ups_terms):
            for r in range(rank // ROWS):
                start = j * rank + r * ROWS
                spot = h * (3 * rank // ROWS) + start // ROWS
                up_terms[spot] = (term[start:start + ROWS] * norm_factor).astype(BF16)

    def one_head(h, carry):
        lanes = pl.ds(pl.multiple_of(h * HEAD, HEAD), HEAD)
        own_rows(h, lanes)
        arrive(h, 0)
        arrive(h, 1)
        for s, (low, got) in enumerate(((low_swap, swap_ref), (low_relay, relay_ref))):
            add = dot_nn(low[...], ups[h, :, HEAD:])
            span = slice((s + 1) * rows, (s + 2) * rows)
            kl[span, 0:HEAD] = (got[h, 0].astype(F32) + add[:, 0:HEAD]).astype(BF16)
            vl[span, 0:HEAD] = (got[h, 1].astype(F32) + add[:, HEAD:]).astype(BF16)
        for t in range(rows // TILE):
            score_grads(t, lanes, softmax(t))
            if t == 1:
                pump(jnp.minimum(h * PARTS + AHEAD, chunks - 2))
        pump(jnp.minimum(h * PARTS + AHEAD + 1, chunks - 1))
        key_sums(lanes)
        value_sums(lanes)
        outputs(h, lanes)
        for part in (2, 3):
            pump_next(h, part)
        return carry

    lax.fori_loop(0, heads - 1, one_head, 0)
    if early_tiles:
        early.terms[0:early_tiles] = up_terms[0:early_tiles]
        early.pair_start()
    else:
        early_out[...] = jnp.zeros_like(early_out)
    last = heads - 1
    lanes = slice(last * HEAD, heads * HEAD)
    own_rows(last, lanes)

    def rebuild(dst, part):
        for s, (low, got) in enumerate(((low_swap, swap_ref), (low_relay, relay_ref))):
            add = dot_nn(low[...], ups[last, :, (part + 1) * HEAD:(part + 2) * HEAD])
            dst[(s + 1) * rows:(s + 2) * rows, 0:HEAD] = (
                got[last, part].astype(F32) + add).astype(BF16)

    arrive(last, 0)
    rebuild(kl, 0)
    for t in range(rows // TILE):
        probs_f[t * TILE:(t + 1) * TILE, :] = softmax(t)
    value_sums(lanes)
    send_back(value_return, rank)
    arrive(last, 1)
    rebuild(vl, 1)
    for t in range(rows // TILE):
        score_grads(t, lanes, probs_f[t * TILE:(t + 1) * TILE, :])
    key_sums(lanes)
    send_back(key_return, 0)
    if early_tiles:
        early.xy_start()
    outputs(last, lanes)

    def down_dot(total, grads, count):
        def columns(i, carry):
            lanes = pl.ds(pl.multiple_of(i * 2 * LANES, 2 * LANES), 2 * LANES)
            term = dot_nn(grads, x_ref[:, lanes]) * norm_factor
            for l in range(2):
                for r in range(count):
                    total.terms[(i * 2 + l) * count + r] = (
                        term[r * ROWS:(r + 1) * ROWS, l * LANES:(l + 1) * LANES].astype(BF16))
            return carry

        lax.fori_loop(0, width // (2 * LANES), columns, 0)

    one = (rank // ROWS) * (width // LANES)
    later.terms[one:counts[2]] = up_terms[early_tiles:]
    grads = jnp.concatenate([rq_ref[...].astype(BF16), take_back(value_return, rank)], axis=0)
    down_dot(first, grads, 2 * rank // ROWS)
    first.pair_start()
    if early_tiles:
        early.z_start()
    grads = take_back(key_return, 0)
    down_dot(later, grads, rank // ROWS)
    later.pair_start()
    first.xy_start()
    if early_tiles:
        early.z_back()
    later.xy_start()
    first.z_start()
    if early_tiles:
        early.xy_back()
    later.z_start()
    first.z_back()
    if early_tiles:
        early.pair_back()
    later.z_back()
    first.xy_back()
    later.xy_back()
    first.pair_back()
    later.pair_back()
    if early_tiles:
        early.finish()
    first.finish()
    later.finish()

    for g in range(2):
        low_copy(g).wait_send()

    @pl.when(relay_out)
    def _():
        for g in range(2):
            low_next(g).wait_send()

    def swap_sent(h, carry):
        for part in range(PARTS):
            swap(h, part).wait_send()
        return carry

    lax.fori_loop(0, heads, swap_sent, 0)

    @pl.when(relay_out)
    def _():
        lax.fori_loop(0, chunks, lambda c, carry: (relay(c).wait_send(), carry)[1], 0)

    for ready in (value_return, key_return):
        ready(0).wait_send()

    @pl.when(relay_in)
    def _():
        for ready in (value_return, key_return):
            ready(1).wait_send()

    lax.fori_loop(0, heads, lambda h, carry: (att_copy(h).wait(), carry)[1], 0)
    early.drain()
    first.drain()
    later.drain()


def fused(nb, nt, norm_factor, step, window, hidden, modulation, down, up, fq, fk, fv, g):
    _, rows, width = hidden.shape
    across = fq.shape[2]
    heads = across // HEAD
    rank = up.shape[0] // 3
    dma = pltpu.SemaphoreType.DMA
    vmem = pltpu.VMEM
    smem = pl.BlockSpec(memory_space=pltpu.SMEM)
    anywhere = pl.BlockSpec(memory_space=pl.ANY)
    whole = pl.BlockSpec(memory_space=pltpu.VMEM)
    chunks = PARTS * heads
    blocks = rows // TILE
    counts = [max(tiles, 1) for tiles in split_tiles(rank, width, heads, nb, nt)]
    totals = [share_of(tiles, nb, nt) * nb * nt for tiles in counts]
    return pl.pallas_call(
        functools.partial(fused_kernel, nb, nt, rank, norm_factor),
        out_shape=[
            jax.ShapeDtypeStruct((1, rows, across), BF16),
        ] + [jax.ShapeDtypeStruct((total, ROWS, LANES), BF16) for total in totals],
        in_specs=[smem, smem] + [anywhere] * 8,
        out_specs=[anywhere, whole, whole, whole],
        scratch_shapes=[
            vmem((rows, width), BF16), vmem(modulation.shape, F32), vmem((2, width), F32),
            vmem((LANES, width), BF16), vmem(up.shape, BF16), vmem((heads, LANES, 3 * HEAD), BF16),
            vmem(fq.shape, BF16), vmem(fq.shape, BF16), vmem(fq.shape, BF16), vmem(fq.shape, BF16),
            vmem((heads, 2, rows, HEAD), BF16), vmem((heads, 2, rows, HEAD), BF16),
            vmem((2, rows // 4, LANES), BF16), vmem((4, rows // 4, LANES), BF16),
            vmem((rows, LANES), BF16), vmem((rows, LANES), BF16), vmem((rows, LANES), BF16),
            vmem((8, 3 * rows), F32), vmem((rows, HEAD), BF16),
            vmem((3 * rows, 2 * HEAD), BF16), vmem((3 * rows, 2 * HEAD), BF16),
            vmem((rows, 3 * rows), F32),
            vmem((rows, 3 * rows), BF16), vmem((rows, 3 * rows), BF16),
            vmem((2 * rank, 3 * rows), F32), vmem((rank, rows), F32),
            vmem((4, rank, rows), BF16), vmem((4, rank, rows), BF16),
            vmem((heads, rows, HEAD), BF16), vmem((heads * (3 * rank // ROWS), ROWS, LANES), BF16),
            dma((blocks + 7,)), dma((heads,)),
            dma((chunks,)), dma((chunks,)), dma((chunks,)), dma((chunks,)),
            dma((4,)), dma((4,)), dma((4,)), dma((4,)),
        ] + sum([sum_shapes(tiles, nb, nt) for tiles in counts], []),
        compiler_params=pltpu.CompilerParams(
            collective_id=0, has_side_effects=True, vmem_limit_bytes=60 << 20
        ),
        name="fused",
    )(step, window, hidden, modulation, down, up, fq, fk, fv, g)


def place_kernel(rank, early_tiles, att_hbm, early_hbm, first_hbm, later_hbm,
                 att_out, down_out, up_out, att_ref, early_ref, first_ref, later_ref, down_ref, up_ref, load, store):
    rows, across = att_ref.shape[1:]
    heads = across // HEAD
    width = down_ref.shape[1]
    one = (rank // ROWS) * (width // LANES)
    parts = 4
    cut = rows // parts
    takes = [pltpu.make_async_copy(first_hbm, first_ref, load.at[0]),
             pltpu.make_async_copy(later_hbm, later_ref, load.at[1]),
             pltpu.make_async_copy(early_hbm, early_ref, load.at[6])]
    moves = [(pltpu.make_async_copy(att_hbm.at[:, pl.ds(i * cut, cut)],
                                    att_ref.at[:, pl.ds(i * cut, cut)], load.at[2 + i]),
              pltpu.make_async_copy(att_ref.at[:, pl.ds(i * cut, cut)],
                                    att_out.at[:, pl.ds(i * cut, cut)], store.at[2 + i]))
             for i in range(parts)]
    for copy in takes:
        copy.start()
    for copy, _ in moves:
        copy.start()
    for copy in takes:
        copy.wait()
    step = rank // ROWS
    for l in range(width // LANES):
        lanes = slice(l * LANES, (l + 1) * LANES)
        for r in range(step):
            spots = (first_ref[l * 2 * step + r], later_ref[l * step + r],
                     first_ref[l * 2 * step + step + r])
            for j, tile in enumerate(spots):
                down_ref[j * rank + r * ROWS:j * rank + (r + 1) * ROWS, lanes] = tile.astype(F32)
    down_store = pltpu.make_async_copy(down_ref, down_out, store.at[0])
    down_store.start()
    for h in range(heads):
        lanes = slice(h * HEAD, (h + 1) * HEAD)
        for r in range(3 * step):
            k = h * 3 * step + r
            tile = early_ref[k] if k < early_tiles else later_ref[one + k - early_tiles]
            up_ref[r * ROWS:(r + 1) * ROWS, lanes] = tile.astype(F32)
    up_store = pltpu.make_async_copy(up_ref, up_out, store.at[1])
    up_store.start()
    for copy, then in moves:
        copy.wait()
        then.start()
    for _, then in moves:
        then.wait()
    down_store.wait()
    up_store.wait()


def put_in_place(rank, width, early_tiles, attended, early, first, later):
    across = attended.shape[2]
    vmem, dma = pltpu.VMEM, pltpu.SemaphoreType.DMA
    anywhere = pl.BlockSpec(memory_space=pl.ANY)
    return pl.pallas_call(
        functools.partial(place_kernel, rank, early_tiles),
        out_shape=[
            jax.ShapeDtypeStruct(attended.shape, BF16),
            jax.ShapeDtypeStruct((3 * rank, width), F32),
            jax.ShapeDtypeStruct((3 * rank, across), F32),
        ],
        in_specs=[anywhere] * 4,
        out_specs=[anywhere] * 3,
        scratch_shapes=[
            vmem(attended.shape, BF16), vmem(early.shape, BF16), vmem(first.shape, BF16), vmem(later.shape, BF16),
            vmem((3 * rank, width), F32), vmem((3 * rank, across), F32), dma((7,)), dma((6,)),
        ],
        name="place",
    )(attended, early, first, later)


def per_device(
    hidden,
    frozen_queries,
    frozen_keys,
    frozen_values,
    reward_output_gradient,
    truncation_step,
    modulation,
    adapter_down_weight,
    adapter_up_weight,
    window,
):
    slab_rows, width = hidden.shape[1:]
    across = frozen_queries.shape[2]
    rank = adapter_up_weight.shape[1]
    nb, nt = lax.axis_size("batch"), lax.axis_size("tiles")
    norm_factor = 1.0 / math.sqrt(hidden.shape[0] * nb * slab_rows * nt)
    down = adapter_down_weight.transpose(0, 2, 1).reshape(3 * rank, width)
    up = adapter_up_weight.reshape(3 * rank, across)
    heads = across // HEAD
    early_tiles = split_tiles(rank, width, heads, nb, nt)[0]
    attended, early, first, later = fused(
        nb, nt, norm_factor, truncation_step, window, hidden, modulation, down, up,
        frozen_queries, frozen_keys, frozen_values, reward_output_gradient,
    )
    attended, grad_down, grad_up = put_in_place(
        rank, width, early_tiles, attended, early, first, later
    )
    grad_down = grad_down.reshape(3, rank, width).transpose(0, 2, 1)
    grad_up = grad_up.reshape(3, rank, across)
    return (attended, grad_down, grad_up)


def solution(mesh):
    placed = (
        P("batch", "tiles", None),
        P("batch", "tiles", None),
        P("batch", "tiles", None),
        P("batch", "tiles", None),
        P("batch", "tiles", None),
        P("batch"),
        P(),
        P(),
        P(),
        P("tiles", None),
    )
    return jax.shard_map(
        per_device,
        mesh=mesh,
        in_specs=placed,
        out_specs=(P("batch", "tiles", None), P(), P()),
        check_vma=False,
    )
```

```python
import functools
import math

import jax
import jax.numpy as jnp
from jax import lax
from jax.experimental import pallas as pl
from jax.experimental.pallas import tpu as pltpu
from jax.sharding import PartitionSpec as P

HEAD = 128
TILE = 128
GF = 2
GR = 2
LANES = 128
ROWS = 16
PARTS = 4
EARLY = 4
AHEAD = 7
BF16 = jnp.bfloat16
F32 = jnp.float32


def dot_nt(a, b):
    return lax.dot_general(
        a, b, (((1,), (1,)), ((), ())), preferred_element_type=jnp.float32
    )


def dot_tn(a, b):
    return lax.dot_general(
        a, b, (((0,), (0,)), ((), ())), preferred_element_type=jnp.float32
    )


def dot_nn(a, b):
    return jnp.dot(a, b, preferred_element_type=jnp.float32)


def remote(src, dst, send, recv, peer):
    return pltpu.make_async_remote_copy(
        src_ref=src, dst_ref=dst, send_sem=send, recv_sem=recv,
        device_id=peer, device_id_type=pl.DeviceIdType.MESH,
    )


class Place:
    def __init__(self, nb, nt):
        self.nb, self.nt = nb, nt
        self.nx, self.nz = nb // 2, nt // 2
        self.nxy = 2 * self.nx
        b, t = lax.axis_index("batch"), lax.axis_index("tiles")
        self.b, self.t = b, t
        self.core, self.x = lax.rem(b, 2), b // 2
        self.y, self.z = lax.rem(t, 2), t // 2

    def core_peer(self):
        return {"batch": self.b + 1 - 2 * self.core}

    def xy_offset(self, d, sign):
        dx, dy = d // 2, d % 2
        x = lax.rem(self.x + sign * dx + self.nx, self.nx)
        return x, lax.rem(self.y + dy, 2)

    def xy_peer(self, d):
        x, y = self.xy_offset(d, 1)
        return {"batch": x * 2 + self.core, "tiles": self.z * 2 + y}

    def xy_index(self, d, sign):
        x, y = self.xy_offset(d, sign)
        return x * 2 + y

    def z_peer(self, e):
        return {"tiles": lax.rem(self.z + e, self.nz) * 2 + self.y}


def share_of(tiles, nb, nt):
    return -(-tiles // (nb * nt))


def split_tiles(rank, width, heads, nb, nt):
    one = (rank // ROWS) * (width // LANES)
    ups = (3 * rank // ROWS) * heads
    early = (ups - 3 * rank // ROWS) // (nb * nt) * (nb * nt)
    return early, 2 * one, one + ups - early


def sum_shapes(tiles, nb, nt):
    share = share_of(tiles, nb, nt)
    nxy, nz = nb, nt // 2
    quarter = nz * share
    total = nb * nt * share
    dma = pltpu.SemaphoreType.DMA
    return [
        pltpu.VMEM((total, ROWS, LANES), BF16),
        pltpu.VMEM((total // 2, ROWS, LANES), BF16),
        pltpu.VMEM((nxy - 1, quarter, ROWS, LANES), BF16),
        pltpu.VMEM((nxy - 1, quarter, ROWS, LANES), BF16),
        pltpu.VMEM((quarter, ROWS, LANES), F32),
        pltpu.VMEM((nz - 1, share, ROWS, LANES), BF16),
        pltpu.VMEM((nz - 1, share, ROWS, LANES), BF16),
        dma((nxy,)), dma((nxy,)), dma((nxy - 1,)), dma((nxy - 1,)),
        dma((nz - 1,)), dma((nz - 1,)), dma((nz - 1,)), dma((nz - 1,)),
        dma((nxy - 1, nz)), dma((nxy - 1, nz)), dma((nxy, nz)), dma((nxy, nz)),
    ]


class Sum:
    def __init__(self, place, tiles, out, refs):
        self.place, self.tiles, self.out = place, tiles, out
        (self.terms, self.pair, self.part1, self.got1, self.acc, self.part2, self.got2,
         self.s0, self.r0, self.s1, self.r1, self.s2, self.r2, self.s3, self.r3,
         self.s4, self.r4, self.s5, self.r5) = refs
        self.share = share_of(tiles, place.nb, place.nt)
        self.quarter = place.nz * self.share
        self.half = place.nxy * self.quarter
        self.mine = place.core * self.half
        self.order = list(range(place.nxy - 1, -1, -1))
        self.sent = []

    def clear(self):
        pad = self.terms.shape[0] - self.tiles
        if pad:
            self.terms[self.tiles:] = jnp.zeros((pad, ROWS, LANES), BF16)

    def go(self, *args):
        copy = remote(*args)
        copy.start()
        self.sent.append(copy)
        return copy

    def pair_start(self):
        p = self.place
        other = (1 - p.core) * self.half
        self.c0 = {}
        for d in self.order:
            q = p.xy_index(d, 1) * self.quarter
            self.c0[d] = self.go(self.terms.at[pl.ds(other + q, self.quarter)],
                                 self.pair.at[pl.ds(q, self.quarter)],
                                 self.s0.at[d], self.r0.at[d], p.core_peer())

    def xy_start(self):
        p = self.place
        self.c1 = {}
        for d in self.order:
            q = p.xy_index(d, 1) * self.quarter
            self.c0[d].wait_recv()
            total = (self.terms[pl.ds(self.mine + q, self.quarter)].astype(F32)
                     + self.pair[pl.ds(q, self.quarter)].astype(F32))
            if d == 0:
                self.acc[...] = total
            else:
                self.part1[d - 1] = total.astype(BF16)
                self.c1[d] = self.go(self.part1.at[d - 1], self.got1.at[d - 1],
                                     self.s1.at[d - 1], self.r1.at[d - 1], p.xy_peer(d))

    def z_start(self):
        p = self.place
        for d in self.order:
            if d:
                self.c1[d].wait_recv()
        total = self.acc[...]
        for d in range(1, p.nxy):
            total = total + self.got1[d - 1].astype(F32)
        self.acc[...] = total
        self.c2 = []
        for e in range(1, p.nz):
            spot = lax.rem(p.z + e, p.nz) * self.share
            self.part2[e - 1] = self.acc[pl.ds(spot, self.share)].astype(BF16)
            self.c2.append(self.go(self.part2.at[e - 1], self.got2.at[e - 1],
                                   self.s2.at[e - 1], self.r2.at[e - 1], p.z_peer(e)))

    def spot(self, d, e):
        p = self.place
        plane = lax.rem(p.z - e + p.nz, p.nz) * self.share
        return self.out.at[pl.ds(self.mine + p.xy_index(d, -1) * self.quarter + plane, self.share)]

    def z_back(self):
        p = self.place
        total = self.acc[pl.ds(p.z * self.share, self.share)]
        for e in range(1, p.nz):
            self.c2[e - 1].wait_recv()
            total = total + self.got2[e - 1].astype(F32)
        mine = self.spot(0, 0)
        mine[...] = total.astype(BF16)
        self.c3 = [self.go(mine, mine, self.s3.at[e - 1], self.r3.at[e - 1], p.z_peer(e))
                   for e in range(1, p.nz)]

    def xy_back(self):
        p = self.place
        self.c4, self.c5 = {}, []
        for e in range(p.nz):
            if e:
                self.c3[e - 1].wait_recv()
            piece = self.spot(0, e)
            for d in self.order:
                if d:
                    self.c4[d, e] = self.go(piece, piece, self.s4.at[d - 1, e],
                                            self.r4.at[d - 1, e], p.xy_peer(d))
            self.c5.append(self.go(piece, piece, self.s5.at[0, e], self.r5.at[0, e],
                                   p.core_peer()))

    def pair_back(self):
        p = self.place
        for e in range(p.nz):
            for d in range(1, p.nxy):
                self.c4[d, e].wait_recv()
                piece = self.spot(d, e)
                self.c5.append(self.go(piece, piece, self.s5.at[d, e], self.r5.at[d, e],
                                       p.core_peer()))

    def finish(self):
        for copy in self.c5:
            copy.wait_recv()

    def drain(self):
        for copy in self.sent:
            copy.wait_send()


def fused_kernel(nb, nt, rank, norm_factor, step_ref, window_ref, hidden_hbm, mod_hbm, down_hbm, up_hbm,
                 fq_hbm, fk_hbm, fv_hbm, g_hbm,
                 att_hbm, early_out, first_out, later_out,
                 x_ref, mod_all, mod_ref, down_ref, up_ref, ups, fq_ref, fk_ref, fv_ref, g_ref,
                 swap_ref, relay_ref, low_pack, low_got, low_ref, low_swap, low_relay, bias_ref, q_ref, kl, vl,
                 probs_f, probs_s, grad_s, rkv, rq_ref, r_out, r_in, att_ref, up_terms,
                 load, att_sem, swap_send, swap_recv, relay_send, relay_recv,
                 low_send, low_recv, r_send, r_recv, *sums):
    place = Place(nb, nt)
    t_index, odd = place.t, place.y
    rows, across = fq_ref.shape[1:]
    heads = across // HEAD
    width = x_ref.shape[1]
    half = rows // 2
    chunks = PARTS * heads
    per = len(sums) // 3
    counts = split_tiles(rank, width, heads, nb, nt)
    outs = (early_out, first_out, later_out)
    early, first, later = [Sum(place, counts[i], outs[i], sums[i * per:(i + 1) * per])
                           for i in range(3)]
    early_tiles = counts[0]

    partner = {"tiles": t_index + 1 - 2 * odd}
    target = {"tiles": lax.rem(t_index + 2 - 4 * odd + nt, nt)}
    other = {"tiles": lax.rem(t_index - 1 + 2 * odd + nt, nt)}
    even = odd == 0
    relay_in = jnp.where(even, t_index >= 2, t_index < nt - 2)
    relay_out = jnp.where(even, t_index < nt - 2, t_index >= 2)

    blocks = rows // TILE
    block = TILE
    hidden_loads = [
        pltpu.make_async_copy(hidden_hbm.at[0, pl.ds(i * block, block)],
                              x_ref.at[pl.ds(i * block, block)], load.at[i])
        for i in range(blocks)
    ]
    others = [
        pltpu.make_async_copy(src, dst, load.at[blocks + i])
        for i, (src, dst) in enumerate((
            (mod_hbm, mod_all), (down_hbm, down_ref.at[pl.ds(0, 3 * rank)]),
            (up_hbm, up_ref),
            (fq_hbm, fq_ref), (fk_hbm, fk_ref), (fv_hbm, fv_ref), (g_hbm, g_ref)))
    ]

    barrier = pltpu.get_barrier_semaphore()
    greet = [place.core_peer(), other]
    greet += [place.xy_peer(d) for d in range(1, place.nxy)]
    greet += [place.z_peer(e) for e in range(1, place.nz)]
    for peer in greet:
        pl.semaphore_signal(barrier, inc=1, device_id=peer, device_id_type=pl.DeviceIdType.MESH)
    hidden_loads[0].start()
    for copy in others[:2]:
        copy.start()
    for copy in hidden_loads[1:]:
        copy.start()

    scale_root = 1.0 / math.sqrt(HEAD)
    scale_two = scale_root * math.log2(math.e)
    per_slab = GF * GR
    sides = (jnp.int32(9), 18 * (1 - odd), 18 * odd)
    for s, side in enumerate(sides):
        for t in range(per_slab):
            for u in range(per_slab):
                code = side + 3 * (u // GR - t // GR + 1) + u % GR - t % GR + 1
                value = jnp.where(window_ref[t, code] > 0, 0.0, -1e30).astype(F32)
                if s == 2:
                    value = jnp.where(relay_in, value, -1e30)
                spot = (s * per_slab + u) * TILE
                bias_ref[t:t + 1, spot:spot + TILE] = jnp.full((1, TILE), value, F32)

    pl.semaphore_wait(barrier, len(greet))

    def swap(h, part):
        src = (fk_hbm, fv_hbm)[part // 2]
        start = (part % 2) * half
        lanes = pl.ds(pl.multiple_of(h * HEAD, HEAD), HEAD)
        c = h * PARTS + part
        return remote(src.at[0, pl.ds(start, half), lanes],
                      swap_ref.at[h, part // 2, pl.ds(start, half)],
                      swap_send.at[c], swap_recv.at[c], partner)

    def chunk(ref, c):
        return ref.at[c // PARTS, lax.rem(c, PARTS) // 2, pl.ds(lax.rem(c, 2) * half, half)]

    def relay(c):
        return remote(chunk(swap_ref, c), chunk(relay_ref, c), relay_send.at[c], relay_recv.at[c],
                      target)

    def pump(c):
        remote(chunk(swap_ref, c), chunk(swap_ref, c), swap_send.at[c], swap_recv.at[c],
               partner).wait_recv()

        @pl.when(relay_out)
        def _():
            relay(c).start()

    for c in range(EARLY):
        swap(c // PARTS, c % PARTS).start()

    @pl.when(jnp.logical_not(relay_in))
    def _():
        low_relay[...] = jnp.zeros_like(low_relay)

        def clear(h, carry):
            relay_ref[h] = jnp.zeros(relay_ref.shape[1:], BF16)
            return carry

        lax.fori_loop(0, heads, clear, 0)
        for j in range(2):
            r_in[2 * j + 1] = jnp.zeros(r_in.shape[1:], BF16)

    early.clear()
    first.clear()
    later.clear()
    rq_ref[...] = jnp.zeros_like(rq_ref)
    rkv[...] = jnp.zeros_like(rkv)
    ups[...] = jnp.zeros_like(ups)
    down_ref[3 * rank:LANES] = jnp.zeros((LANES - 3 * rank, width), BF16)

    for copy in others[:2]:
        copy.wait()
    mod_ref[...] = mod_all[step_ref[0]]
    row = lax.broadcasted_iota(jnp.int32, (LANES, LANES), 0)
    lane = lax.broadcasted_iota(jnp.int32, (LANES, LANES), 1)
    wide = 2 * rank

    def low_copy(g):
        return remote(low_pack.at[g], low_got.at[g], low_send.at[g], low_recv.at[g], partner)

    def low_next(g):
        return remote(low_got.at[g], low_got.at[2 + g], low_send.at[2 + g], low_recv.at[2 + g],
                      target)

    def one_hot(pick):
        return jnp.where(pick, 1.0, 0.0).astype(BF16)

    def pack_low(g):
        total = jnp.zeros((rows // 4, LANES), F32)
        for part in range(2):
            pick = jnp.logical_and(lane // wide == part, row - rank == lane - part * wide)
            start = (2 * g + part) * (rows // 4)
            total = total + dot_nn(low_ref[start:start + rows // 4, :], one_hot(pick))
        low_pack[g] = total.astype(BF16)
        low_copy(g).start()

    def modulate(i, carry):
        span = pl.ds(pl.multiple_of(i * block, block), block)
        pltpu.make_async_copy(hidden_hbm.at[0, span], x_ref.at[span], load.at[i]).wait()
        x = x_ref[span, :].astype(F32)
        mean = jnp.sum(x, axis=1, keepdims=True) * (1.0 / width)
        centred = x - mean
        variance = jnp.sum(centred * centred, axis=1, keepdims=True) * (1.0 / width)
        normed = centred * lax.rsqrt(variance + 1e-06)
        x_low = (normed * (1.0 + mod_ref[1:2, :]) + mod_ref[0:1, :]).astype(BF16)
        x_ref[span, :] = x_low
        low_ref[span, :] = dot_nt(x_low, down_ref[...]).astype(BF16)
        return carry

    half_blocks = blocks // 2
    lax.fori_loop(0, half_blocks, modulate, 0)
    pack_low(0)
    lax.fori_loop(half_blocks, blocks - 1, modulate, 0)
    pump(0)
    lax.fori_loop(blocks - 1, blocks, modulate, 0)
    pack_low(1)
    for c in range(EARLY, 2 * PARTS):
        swap(c // PARTS, c % PARTS).start()

    def send_rest(h, carry):
        for part in range(PARTS):
            swap(h, part).start()
        return carry

    lax.fori_loop(2, heads, send_rest, 0)
    for copy in others[2:]:
        copy.start()
    pump(1)
    for copy in others[2:]:
        copy.wait()

    def build(h, carry):
        lanes = pl.ds(pl.multiple_of(h * HEAD, HEAD), HEAD)
        for j in range(3):
            ups[h, j * rank:(j + 1) * rank, j * HEAD:(j + 1) * HEAD] = (
                up_ref[j * rank:(j + 1) * rank, lanes])
        return carry

    lax.fori_loop(0, heads, build, 0)
    pump(2)
    pump(3)
    for g in range(2):
        low_copy(g).wait_recv()

        @pl.when(relay_out)
        def _(g=g):
            low_next(g).start()

    inside = jnp.logical_and(lane >= rank, lane < 3 * rank)

    def unpack_low(s, dst):
        quarter = rows // 4
        for part in range(2):
            pick = jnp.logical_and(inside, row == lane - rank + part * wide)
            select = one_hot(pick)
            for g in range(2):
                start = (2 * g + part) * quarter
                dst[start:start + quarter, :] = dot_nn(low_got[2 * s + g], select).astype(BF16)

    unpack_low(0, low_swap)
    for c in range(PARTS, AHEAD):
        pump(c)

    @pl.when(relay_in)
    def _():
        for g in range(2):
            low_next(g).wait_recv()
        unpack_low(1, low_relay)

    def value_return(s):
        return remote(r_out.at[s], r_in.at[s], r_send.at[s], r_recv.at[s], (partner, other)[s])

    def key_return(s):
        return remote(r_out.at[2 + s], r_in.at[2 + s], r_send.at[2 + s], r_recv.at[2 + s],
                      (partner, other)[s])

    def send_back(ready, start):
        base = 0 if ready is value_return else 2
        for s in range(2):
            r_out[base + s] = rkv[start:start + rank, (s + 1) * rows:(s + 2) * rows].astype(BF16)
        ready(0).start()

        @pl.when(relay_in)
        def _():
            ready(1).start()

    def take_back(ready, start):
        base = 0 if ready is value_return else 2
        ready(0).wait_recv()

        @pl.when(relay_in)
        def _():
            ready(1).wait_recv()

        return (rkv[start:start + rank, 0:rows] + r_in[base].astype(F32)
                + r_in[base + 1].astype(F32)).astype(BF16)

    for s, low in enumerate((low_ref, low_swap, low_relay)):
        kl[s * rows:(s + 1) * rows, HEAD:] = low[...]
        vl[s * rows:(s + 1) * rows, HEAD:] = low[...]


    def att_copy(h):
        lanes = pl.ds(pl.multiple_of(h * HEAD, HEAD), HEAD)
        return pltpu.make_async_copy(att_ref.at[h], att_hbm.at[0, :, lanes], att_sem.at[h])

    def pump_next(h, part):
        c = h * PARTS + AHEAD + part

        @pl.when(c < chunks - 2)
        def _():
            pump(c)

    def arrive(h, part):
        @pl.when(relay_in)
        def _():
            for i in range(2):
                relay(h * PARTS + 2 * part + i).wait_recv()

    def own_rows(h, lanes):
        own = dot_nn(low_ref[...], ups[h])
        q_ref[...] = (fq_ref[0, :, lanes].astype(F32) + own[:, 0:HEAD]).astype(BF16)
        kl[0:rows, 0:HEAD] = (fk_ref[0, :, lanes].astype(F32) + own[:, HEAD:2 * HEAD]).astype(BF16)
        vl[0:rows, 0:HEAD] = (fv_ref[0, :, lanes].astype(F32) + own[:, 2 * HEAD:]).astype(BF16)

    def softmax(t):
        span = slice(t * TILE, (t + 1) * TILE)
        scores = dot_nt(q_ref[span, :], kl[:, 0:HEAD]) * scale_two + bias_ref[t:t + 1, :]
        top = jnp.max(scores, axis=1, keepdims=True)
        weights = jnp.exp2(scores - top)
        inverse = 1.0 / jnp.sum(weights, axis=1, keepdims=True)
        probs = weights * inverse
        probs_s[span, :] = probs.astype(BF16)
        return probs

    def score_grads(t, lanes, probs):
        span = slice(t * TILE, (t + 1) * TILE)
        prob_grad = dot_nt(g_ref[0, span, lanes], vl[:, 0:HEAD])
        centre = jnp.sum(probs * prob_grad, axis=1, keepdims=True)
        grad_s[span, :] = (probs * (prob_grad - centre) * scale_root).astype(BF16)

    def key_sums(lanes):
        q_up = dot_nt(up_ref[rank:2 * rank, lanes], q_ref[...]).astype(BF16)
        rkv[0:rank, :] += dot_nn(q_up, grad_s[...])

    def value_sums(lanes):
        g_up = dot_nt(up_ref[2 * rank:3 * rank, lanes], g_ref[0, :, lanes]).astype(BF16)
        rkv[rank:2 * rank, :] += dot_nn(g_up, probs_s[...])

    def outputs(h, lanes):
        q_all = q_ref[...]
        g_all = g_ref[0, :, lanes]
        att = dot_nn(probs_s[...], vl[...])
        att_ref[h] = att[:, 0:HEAD].astype(BF16)
        att_copy(h).start()
        low_v = att[:, HEAD:].astype(BF16)
        dq = dot_nn(grad_s[...], kl[...])
        dq_low = dq[:, 0:HEAD].astype(BF16)
        low_k = dq[:, HEAD:].astype(BF16)
        rq_ref[...] += dot_nt(up_ref[0:rank, lanes], dq_low)
        ups_terms = (dot_tn(low_ref[...], dq_low), dot_tn(low_k, q_all), dot_tn(low_v, g_all))
        for j, term in enumerate(ups_terms):
            for r in range(rank // ROWS):
                start = j * rank + r * ROWS
                spot = h * (3 * rank // ROWS) + start // ROWS
                up_terms[spot] = (term[start:start + ROWS] * norm_factor).astype(BF16)

    def one_head(h, carry):
        lanes = pl.ds(pl.multiple_of(h * HEAD, HEAD), HEAD)
        own_rows(h, lanes)
        arrive(h, 0)
        arrive(h, 1)
        for s, (low, got) in enumerate(((low_swap, swap_ref), (low_relay, relay_ref))):
            add = dot_nn(low[...], ups[h, :, HEAD:])
            span = slice((s + 1) * rows, (s + 2) * rows)
            kl[span, 0:HEAD] = (got[h, 0].astype(F32) + add[:, 0:HEAD]).astype(BF16)
            vl[span, 0:HEAD] = (got[h, 1].astype(F32) + add[:, HEAD:]).astype(BF16)
        for t in range(rows // TILE):
            score_grads(t, lanes, softmax(t))
            if t == 1:
                pump(jnp.minimum(h * PARTS + AHEAD, chunks - 2))
        pump(jnp.minimum(h * PARTS + AHEAD + 1, chunks - 1))
        key_sums(lanes)
        value_sums(lanes)
        outputs(h, lanes)
        for part in (2, 3):
            pump_next(h, part)
        return carry

    lax.fori_loop(0, heads - 1, one_head, 0)
    if early_tiles:
        early.terms[0:early_tiles] = up_terms[0:early_tiles]
        early.pair_start()
    else:
        early_out[...] = jnp.zeros_like(early_out)
    last = heads - 1
    lanes = slice(last * HEAD, heads * HEAD)
    own_rows(last, lanes)

    def rebuild(dst, part):
        for s, (low, got) in enumerate(((low_swap, swap_ref), (low_relay, relay_ref))):
            add = dot_nn(low[...], ups[last, :, (part + 1) * HEAD:(part + 2) * HEAD])
            dst[(s + 1) * rows:(s + 2) * rows, 0:HEAD] = (
                got[last, part].astype(F32) + add).astype(BF16)

    arrive(last, 0)
    rebuild(kl, 0)
    for t in range(rows // TILE):
        probs_f[t * TILE:(t + 1) * TILE, :] = softmax(t)
    value_sums(lanes)
    send_back(value_return, rank)
    arrive(last, 1)
    rebuild(vl, 1)
    for t in range(rows // TILE):
        score_grads(t, lanes, probs_f[t * TILE:(t + 1) * TILE, :])
    key_sums(lanes)
    send_back(key_return, 0)
    if early_tiles:
        early.xy_start()
    outputs(last, lanes)

    def down_dot(total, grads, count):
        def columns(i, carry):
            lanes = pl.ds(pl.multiple_of(i * 2 * LANES, 2 * LANES), 2 * LANES)
            term = dot_nn(grads, x_ref[:, lanes]) * norm_factor
            for l in range(2):
                for r in range(count):
                    total.terms[(i * 2 + l) * count + r] = (
                        term[r * ROWS:(r + 1) * ROWS, l * LANES:(l + 1) * LANES].astype(BF16))
            return carry

        lax.fori_loop(0, width // (2 * LANES), columns, 0)

    one = (rank // ROWS) * (width // LANES)
    later.terms[one:counts[2]] = up_terms[early_tiles:]
    grads = jnp.concatenate([rq_ref[...].astype(BF16), take_back(value_return, rank)], axis=0)
    down_dot(first, grads, 2 * rank // ROWS)
    first.pair_start()
    if early_tiles:
        early.z_start()
    grads = take_back(key_return, 0)
    down_dot(later, grads, rank // ROWS)
    later.pair_start()
    first.xy_start()
    later.xy_start()
    if early_tiles:
        early.z_back()
    first.z_start()
    later.z_start()
    if early_tiles:
        early.xy_back()
    first.z_back()
    later.z_back()
    if early_tiles:
        early.pair_back()
    first.xy_back()
    later.xy_back()
    first.pair_back()
    later.pair_back()
    if early_tiles:
        early.finish()
    first.finish()
    later.finish()

    for g in range(2):
        low_copy(g).wait_send()

    @pl.when(relay_out)
    def _():
        for g in range(2):
            low_next(g).wait_send()

    def swap_sent(h, carry):
        for part in range(PARTS):
            swap(h, part).wait_send()
        return carry

    lax.fori_loop(0, heads, swap_sent, 0)

    @pl.when(relay_out)
    def _():
        lax.fori_loop(0, chunks, lambda c, carry: (relay(c).wait_send(), carry)[1], 0)

    for ready in (value_return, key_return):
        ready(0).wait_send()

    @pl.when(relay_in)
    def _():
        for ready in (value_return, key_return):
            ready(1).wait_send()

    lax.fori_loop(0, heads, lambda h, carry: (att_copy(h).wait(), carry)[1], 0)
    early.drain()
    first.drain()
    later.drain()


def fused(nb, nt, norm_factor, step, window, hidden, modulation, down, up, fq, fk, fv, g):
    _, rows, width = hidden.shape
    across = fq.shape[2]
    heads = across // HEAD
    rank = up.shape[0] // 3
    dma = pltpu.SemaphoreType.DMA
    vmem = pltpu.VMEM
    smem = pl.BlockSpec(memory_space=pltpu.SMEM)
    anywhere = pl.BlockSpec(memory_space=pl.ANY)
    whole = pl.BlockSpec(memory_space=pltpu.VMEM)
    chunks = PARTS * heads
    blocks = rows // TILE
    counts = [max(tiles, 1) for tiles in split_tiles(rank, width, heads, nb, nt)]
    totals = [share_of(tiles, nb, nt) * nb * nt for tiles in counts]
    return pl.pallas_call(
        functools.partial(fused_kernel, nb, nt, rank, norm_factor),
        out_shape=[
            jax.ShapeDtypeStruct((1, rows, across), BF16),
        ] + [jax.ShapeDtypeStruct((total, ROWS, LANES), BF16) for total in totals],
        in_specs=[smem, smem] + [anywhere] * 8,
        out_specs=[anywhere, whole, whole, whole],
        scratch_shapes=[
            vmem((rows, width), BF16), vmem(modulation.shape, F32), vmem((2, width), F32),
            vmem((LANES, width), BF16), vmem(up.shape, BF16), vmem((heads, LANES, 3 * HEAD), BF16),
            vmem(fq.shape, BF16), vmem(fq.shape, BF16), vmem(fq.shape, BF16), vmem(fq.shape, BF16),
            vmem((heads, 2, rows, HEAD), BF16), vmem((heads, 2, rows, HEAD), BF16),
            vmem((2, rows // 4, LANES), BF16), vmem((4, rows // 4, LANES), BF16),
            vmem((rows, LANES), BF16), vmem((rows, LANES), BF16), vmem((rows, LANES), BF16),
            vmem((8, 3 * rows), F32), vmem((rows, HEAD), BF16),
            vmem((3 * rows, 2 * HEAD), BF16), vmem((3 * rows, 2 * HEAD), BF16),
            vmem((rows, 3 * rows), F32),
            vmem((rows, 3 * rows), BF16), vmem((rows, 3 * rows), BF16),
            vmem((2 * rank, 3 * rows), F32), vmem((rank, rows), F32),
            vmem((4, rank, rows), BF16), vmem((4, rank, rows), BF16),
            vmem((heads, rows, HEAD), BF16), vmem((heads * (3 * rank // ROWS), ROWS, LANES), BF16),
            dma((blocks + 7,)), dma((heads,)),
            dma((chunks,)), dma((chunks,)), dma((chunks,)), dma((chunks,)),
            dma((4,)), dma((4,)), dma((4,)), dma((4,)),
        ] + sum([sum_shapes(tiles, nb, nt) for tiles in counts], []),
        compiler_params=pltpu.CompilerParams(
            collective_id=0, has_side_effects=True, vmem_limit_bytes=60 << 20
        ),
        name="fused",
    )(step, window, hidden, modulation, down, up, fq, fk, fv, g)


def place_kernel(rank, early_tiles, att_hbm, early_hbm, first_hbm, later_hbm,
                 att_out, down_out, up_out, att_ref, early_ref, first_ref, later_ref, down_ref, up_ref, load, store):
    rows, across = att_ref.shape[1:]
    heads = across // HEAD
    width = down_ref.shape[1]
    one = (rank // ROWS) * (width // LANES)
    parts = 4
    cut = rows // parts
    takes = [pltpu.make_async_copy(first_hbm, first_ref, load.at[0]),
             pltpu.make_async_copy(later_hbm, later_ref, load.at[1]),
             pltpu.make_async_copy(early_hbm, early_ref, load.at[6])]
    moves = [(pltpu.make_async_copy(att_hbm.at[:, pl.ds(i * cut, cut)],
                                    att_ref.at[:, pl.ds(i * cut, cut)], load.at[2 + i]),
              pltpu.make_async_copy(att_ref.at[:, pl.ds(i * cut, cut)],
                                    att_out.at[:, pl.ds(i * cut, cut)], store.at[2 + i]))
             for i in range(parts)]
    for copy in takes:
        copy.start()
    for copy, _ in moves:
        copy.start()
    for copy in takes:
        copy.wait()
    step = rank // ROWS
    for l in range(width // LANES):
        lanes = slice(l * LANES, (l + 1) * LANES)
        for r in range(step):
            spots = (first_ref[l * 2 * step + r], later_ref[l * step + r],
                     first_ref[l * 2 * step + step + r])
            for j, tile in enumerate(spots):
                down_ref[j * rank + r * ROWS:j * rank + (r + 1) * ROWS, lanes] = tile.astype(F32)
    down_store = pltpu.make_async_copy(down_ref, down_out, store.at[0])
    down_store.start()
    for h in range(heads):
        lanes = slice(h * HEAD, (h + 1) * HEAD)
        for r in range(3 * step):
            k = h * 3 * step + r
            tile = early_ref[k] if k < early_tiles else later_ref[one + k - early_tiles]
            up_ref[r * ROWS:(r + 1) * ROWS, lanes] = tile.astype(F32)
    up_store = pltpu.make_async_copy(up_ref, up_out, store.at[1])
    up_store.start()
    for copy, then in moves:
        copy.wait()
        then.start()
    for _, then in moves:
        then.wait()
    down_store.wait()
    up_store.wait()


def put_in_place(rank, width, early_tiles, attended, early, first, later):
    across = attended.shape[2]
    vmem, dma = pltpu.VMEM, pltpu.SemaphoreType.DMA
    anywhere = pl.BlockSpec(memory_space=pl.ANY)
    return pl.pallas_call(
        functools.partial(place_kernel, rank, early_tiles),
        out_shape=[
            jax.ShapeDtypeStruct(attended.shape, BF16),
            jax.ShapeDtypeStruct((3 * rank, width), F32),
            jax.ShapeDtypeStruct((3 * rank, across), F32),
        ],
        in_specs=[anywhere] * 4,
        out_specs=[anywhere] * 3,
        scratch_shapes=[
            vmem(attended.shape, BF16), vmem(early.shape, BF16), vmem(first.shape, BF16), vmem(later.shape, BF16),
            vmem((3 * rank, width), F32), vmem((3 * rank, across), F32), dma((7,)), dma((6,)),
        ],
        name="place",
    )(attended, early, first, later)


def per_device(
    hidden,
    frozen_queries,
    frozen_keys,
    frozen_values,
    reward_output_gradient,
    truncation_step,
    modulation,
    adapter_down_weight,
    adapter_up_weight,
    window,
):
    slab_rows, width = hidden.shape[1:]
    across = frozen_queries.shape[2]
    rank = adapter_up_weight.shape[1]
    nb, nt = lax.axis_size("batch"), lax.axis_size("tiles")
    norm_factor = 1.0 / math.sqrt(hidden.shape[0] * nb * slab_rows * nt)
    down = adapter_down_weight.transpose(0, 2, 1).reshape(3 * rank, width)
    up = adapter_up_weight.reshape(3 * rank, across)
    heads = across // HEAD
    early_tiles = split_tiles(rank, width, heads, nb, nt)[0]
    attended, early, first, later = fused(
        nb, nt, norm_factor, truncation_step, window, hidden, modulation, down, up,
        frozen_queries, frozen_keys, frozen_values, reward_output_gradient,
    )
    attended, grad_down, grad_up = put_in_place(
        rank, width, early_tiles, attended, early, first, later
    )
    grad_down = grad_down.reshape(3, rank, width).transpose(0, 2, 1)
    grad_up = grad_up.reshape(3, rank, across)
    return (attended, grad_down, grad_up)


def solution(mesh):
    placed = (
        P("batch", "tiles", None),
        P("batch", "tiles", None),
        P("batch", "tiles", None),
        P("batch", "tiles", None),
        P("batch", "tiles", None),
        P("batch"),
        P(),
        P(),
        P(),
        P("tiles", None),
    )
    return jax.shard_map(
        per_device,
        mesh=mesh,
        in_specs=placed,
        out_specs=(P("batch", "tiles", None), P(), P()),
        check_vma=False,
    )
```
